256 devices in a mesh: dp: 4 (over x), seq: 8 (over y, core), tensor: 8 (over z).
Axes of the slice: x: 4, y: 4, z: 8, core: 2. Of those that a mesh axis runs over, the one named last changes fastest.
Arguments:
- tokens: bfloat16 [16384, 8192], P(('dp', 'seq'), 'tensor'), may hold values from -6 to 6
- out_grad: bfloat16 [16384, 8192], P(('dp', 'seq'), 'tensor'), may hold values from -6 to 6
- up_perm: int32 [2, 16, 4], replicated, may hold values from 0 to 3, each once within a row
- down_perm: int32 [2, 16, 4], replicated, may hold values from 0 to 3, each once within a row
- up_weight: bfloat16 [64, 2, 256, 256], P('tensor'), may hold values from -0.25 to 0.25
- down_weight: bfloat16 [64, 2, 256, 256], P('tensor'), may hold values from -0.1875 to 0.1875
Outputs:
- output: bfloat16 [16384, 8192], P(('dp', 'seq'), 'tensor')
- input_grad: bfloat16 [16384, 8192], P(('dp', 'seq'), 'tensor')
- grad_up: float32 [64, 2, 256, 256], P('tensor', None, ('dp', 'seq'))
- grad_down: float32 [64, 2, 256, 256], P('tensor', None, ('dp', 'seq'))
The draws below stay inside these ranges and needn't reach their ends.
Inputs may be any that keep to these rules, and one draw needn't show every extreme that they name: `up_perm`: for each section, every run of 4 consecutive entries along the last dimension is a permutation of 0 to 3. `down_perm`: for each section, every run of 4 consecutive entries along the last dimension is a permutation of 0 to 3.
All inputs are finite; a program needn't handle non-finite values.
Results may differ from the reference program's by a relative error of at most 0.0049.
Values may be sent and summed in bfloat16 or wider, within the bound.
A program may use at most 128 MiB of HBM per device.

```python
import jax
import jax.numpy as jnp
from jax import lax

D = 8192
FF = 16384
B = 256
SECTIONS = 2
NB = 32
HB = 64
GROUPS = 8
FPD = 4
HPD = 8
TOKENS = 16384


def block_levels(rng, extent, cuts, least, top_value):
    gain, own = 1.0, jax.random.fold_in(rng, 6)
    for position, blocks in cuts:
        steps = jnp.exp(jax.random.uniform(jax.random.fold_in(own, position), (blocks,), jnp.float32, least / len(cuts), top_value / len(cuts)))
        gain = gain * jnp.repeat(steps, extent[position] // blocks).reshape([-1 if axis == position else 1 for axis in range(len(extent))])
    return gain


def centred(rng, shape, width, limit, shards=(), kind=jnp.bfloat16):
    result = jax.random.normal(rng, shape, jnp.float32) * width
    if len(shards) > 0:
        result = block_levels(rng, shape, shards, -0.22, 0.18) * result
    return jnp.clip(result, min=-limit, max=limit).astype(kind)


def setup_inputs(seed: int = 0) -> dict:
    key_of = jax.random.split(jax.random.key(seed), 7)
    tokens = centred(key_of[0], (TOKENS, D), 1.0, 6.0, ((0, 32), (1, 8)))
    out_grad = centred(key_of[1], (TOKENS, D), 1.0, 6.0, ((0, 32), (1, 8)))
    up_perm = jax.vmap(lambda own: jax.random.permutation(own, FPD))(jax.random.split(key_of[2], SECTIONS * (HB // FPD))).reshape((SECTIONS, HB // FPD, FPD)).astype(jnp.int32)
    down_perm = jax.vmap(lambda own: jax.random.permutation(own, FPD))(jax.random.split(key_of[3], SECTIONS * (HB // FPD))).reshape((SECTIONS, HB // FPD, FPD)).astype(jnp.int32)
    up_weight = centred(key_of[4], (HB, SECTIONS, B, B), (SECTIONS * B) ** -0.5, 0.25, ((0, 8),))
    down_weight = centred(key_of[5], (HB, SECTIONS, B, B), (2 * FF // NB) ** -0.5, 0.1875, ((0, 8),))
    return {"tokens": tokens, "out_grad": out_grad, "up_perm": up_perm, "down_perm": down_perm, "up_weight": up_weight, "down_weight": down_weight}


def block_index(perm_flat, hidx, section_id):
    group_id = hidx // HPD
    paired = (group_id + section_id * (GROUPS // 2)) % GROUPS
    return (paired * FPD + perm_flat[section_id, hidx]).astype(jnp.int32)

def add_block(accum, term, block_id):
    start = (block_id * B).astype(jnp.int32)
    current = lax.dynamic_slice_in_dim(accum, start, B, 1)
    return lax.dynamic_update_slice_in_dim(accum, current + term, start, 1)

def reference(tokens, out_grad, up_perm, down_perm, up_weight, down_weight):
    grad_scale = float(TOKENS) ** (-0.5)
    up_flat = up_perm.reshape(SECTIONS, HB)
    down_flat = down_perm.reshape(SECTIONS, HB)

    def one_block(carry, inputs):
        out_acc, back_acc = carry
        hidx, up_blk, down_blk = inputs
        in_ids = [block_index(up_flat, hidx, 0), block_index(up_flat, hidx, 1)]
        out_ids = [block_index(down_flat, hidx, 0), block_index(down_flat, hidx, 1)]
        in_cols = [lax.dynamic_slice_in_dim(tokens, (blk * B).astype(jnp.int32), B, 1) for blk in in_ids]
        grad_cols = [lax.dynamic_slice_in_dim(out_grad, (blk * B).astype(jnp.int32), B, 1) for blk in out_ids]
        pre_act = jnp.dot(in_cols[0], up_blk[0], preferred_element_type=jnp.float32)
        pre_act = pre_act + jnp.dot(in_cols[1], up_blk[1], preferred_element_type=jnp.float32)
        hidden = jax.nn.gelu(pre_act).astype(jnp.bfloat16)
        out_acc = add_block(out_acc, jnp.dot(hidden, down_blk[0], preferred_element_type=jnp.float32), out_ids[0])
        out_acc = add_block(out_acc, jnp.dot(hidden, down_blk[1], preferred_element_type=jnp.float32), out_ids[1])
        d_hidden = jnp.dot(grad_cols[0], down_blk[0].T, preferred_element_type=jnp.float32)
        d_hidden = d_hidden + jnp.dot(grad_cols[1], down_blk[1].T, preferred_element_type=jnp.float32)
        _, pull_back = jax.vjp(jax.nn.gelu, pre_act)
        d_pre = pull_back(d_hidden)[0].astype(jnp.bfloat16)
        grad_dn = jnp.stack([jnp.dot(hidden.T, grad_cols[0], preferred_element_type=jnp.float32), jnp.dot(hidden.T, grad_cols[1], preferred_element_type=jnp.float32)]) * grad_scale
        grad_upb = jnp.stack([jnp.dot(in_cols[0].T, d_pre, preferred_element_type=jnp.float32), jnp.dot(in_cols[1].T, d_pre, preferred_element_type=jnp.float32)]) * grad_scale
        back_acc = add_block(back_acc, jnp.dot(d_pre, up_blk[0].T, preferred_element_type=jnp.float32), in_ids[0])
        back_acc = add_block(back_acc, jnp.dot(d_pre, up_blk[1].T, preferred_element_type=jnp.float32), in_ids[1])
        return ((out_acc, back_acc), (grad_upb, grad_dn))
    zeros_out = jnp.zeros((TOKENS, D), jnp.float32)
    zeros_back = jnp.zeros((TOKENS, D), jnp.float32)
    hidx_all = jnp.arange(HB, dtype=jnp.int32)
    (out_acc, back_acc), (grad_up, grad_down) = lax.scan(one_block, (zeros_out, zeros_back), (hidx_all, up_weight, down_weight))
    return (out_acc.astype(jnp.bfloat16), back_acc.astype(jnp.bfloat16), grad_up, grad_down)
```

```python
import functools
import math

import jax
import jax.numpy as jnp
from jax import lax
from jax.experimental import pallas as pl
from jax.experimental.pallas import tpu as pltpu
from jax.sharding import PartitionSpec as P

F32 = jnp.float32
BF16 = jnp.bfloat16
B = 256
NF = 4
NH = 8
CHUNKS = 2
ROOT = math.sqrt(2.0 / math.pi)
CUBE = 0.044715


def dot(a, b):
    return jnp.dot(a, b, preferred_element_type=F32)


def dot_nt(a, b):
    return lax.dot_general(a, b, (((1,), (1,)), ((), ())), preferred_element_type=F32)


def lanes(block):
    return pl.ds(pl.multiple_of(block * B, B), B)


def loop(count, body):
    lax.fori_loop(0, count, lambda i, c: (body(i), c)[1], 0)


def kernel(
    sizes, scale,
    table, tok_hbm, grd_hbm, upw_hbm, dnw_hbm,
    out_hbm, ig_hbm, gup_ref, gdn_ref,
    w, tcs, gcs, tt, gj, hid, hidt, dpre, obuf,
    keep, snd, rcv, s1, r1, s2, f2, r2, f3, zs, zr, fx, fr,
    loc_sem, zw_sem, zi_send, zi_recv, ag_send, ag_recv, sb_send, sb_recv,
    zo_send, zo_recv, lo_sem, cs_send, cs_recv, r1_send, r1_recv, r2_send, r2_recv, end_sem,
):
    n_dp, n_seq, n_t = sizes
    n_y = n_seq // 2
    dp, seq, t = lax.axis_index("dp"), lax.axis_index("seq"), lax.axis_index("tensor")
    y, core = seq // 2, lax.rem(seq, 2)
    half = tok_hbm.shape[0] // 2
    rows_c = half // CHUNKS
    upper = t // (n_t // 2)
    keep_off = upper * half
    send_off = half - keep_off

    def peer(d, s, q):
        return {"dp": d, "seq": s, "tensor": q}

    z_peer = peer(dp, seq, lax.rem(t + n_t // 2, n_t))
    sibling = peer(dp, seq + 1 - 2 * core, t)

    def first_peer(k):
        return peer(lax.rem(dp + k * (1 - core), n_dp), lax.rem(seq + 2 * k * core, n_seq), t)

    def second_peer(k):
        return peer(lax.rem(dp + k * core, n_dp), lax.rem(seq + 2 * k * (1 - core), n_seq), t)

    def remote(src, dst, send, recv, device):
        return pltpu.make_async_remote_copy(
            src_ref=src, dst_ref=dst, send_sem=send, recv_sem=recv,
            device_id=device, device_id_type=pl.DeviceIdType.MESH,
        )

    local = [
        pltpu.make_async_copy(upw_hbm, w.at[0, 0], loc_sem.at[0]),
        pltpu.make_async_copy(dnw_hbm, w.at[0, 1], loc_sem.at[1]),
    ]
    for i in range(CHUNKS):
        rows = pl.ds(pl.multiple_of(keep_off + i * rows_c, rows_c), rows_c)
        for j, (src, dst) in enumerate(((tok_hbm, tcs[i]), (grd_hbm, gcs[i]))):
            for f in range(NF):
                n = (2 * i + j) * NF + f
                local.append(
                    pltpu.make_async_copy(src.at[rows, f * B : (f + 1) * B], dst.at[0, f], loc_sem.at[2 + n])
                )
    for copy in local:
        copy.start()

    barrier = pltpu.get_barrier_semaphore()
    greeted = [z_peer, sibling]
    greeted += [first_peer(k) for k in range(1, n_dp)] + [second_peer(k) for k in range(1, n_y)]
    for device in greeted:
        pl.semaphore_signal(barrier, inc=1, device_id=device, device_id_type=pl.DeviceIdType.MESH)
    pl.semaphore_wait(barrier, len(greeted))

    chip = dp * n_y + y
    hrows = pl.ds(pl.multiple_of(core * (B // 2), B // 2), B // 2)

    def unit(u, part=hrows):
        return w.at[1, :, u, part]

    zw = [
        remote(upw_hbm.at[chip, hrows], w.at[1, 0, chip, hrows], zw_sem.at[0], zw_sem.at[1], z_peer),
        remote(dnw_hbm.at[chip, hrows], w.at[1, 1, chip, hrows], zw_sem.at[2], zw_sem.at[3], z_peer),
    ]
    for copy in zw:
        copy.start()
    zi = []
    for i in range(CHUNKS):
        rows = pl.ds(pl.multiple_of(send_off + i * rows_c, rows_c), rows_c)
        for j, (src, dst) in enumerate(((tok_hbm, tcs[i]), (grd_hbm, gcs[i]))):
            for f in range(NF):
                n = (2 * i + j) * NF + f
                zi.append(
                    remote(
                        src.at[rows, f * B : (f + 1) * B], dst.at[1, f], zi_send.at[n], zi_recv.at[n], z_peer
                    )
                )
                zi[-1].start()

    def first_copy(k, u):
        return remote(unit(u), unit(u), ag_send.at[k - 1], ag_recv.at[u], first_peer(k))

    def second_copy(m, k, u):
        return remote(unit(u), unit(u), ag_send.at[3 + 3 * m + k - 1], ag_recv.at[u], second_peer(k))

    def sibling_copy(u):
        return remote(unit(u), unit(u), sb_send.at[u], sb_recv.at[u], sibling)

    other = pl.ds(pl.multiple_of((1 - core) * (B // 2), B // 2), B // 2)

    def sibling_arrival(u):
        return remote(unit(u, other), unit(u, other), sb_send.at[u], sb_recv.at[u], sibling)

    def moved(u_dp, u_y, k1, k2):
        a = lax.rem(u_dp + 8 * n_dp - k1 * (1 - core) - k2 * core, n_dp)
        b = lax.rem(u_y + 8 * n_y - k1 * core - k2 * (1 - core), n_y)
        return a * n_y + b

    for copy in zw:
        copy.wait_recv()
    for k in range(1, n_dp):
        first_copy(k, chip).start()
    for m in range(n_dp):
        u = moved(dp, y, m, 0)
        if m:
            first_copy(m, u).wait_recv()
        for k in range(1, n_y):
            second_copy(m, k, u).start()
        sibling_copy(u).start()
    for k in range(1, n_y):
        for m in range(n_dp):
            u = moved(dp, y, m, k)
            second_copy(m, k, u).wait_recv()
            sibling_copy(u).start()
    for copy in local:
        copy.wait()
    loop(n_dp * n_y, lambda u: sibling_arrival(u).wait_recv())

    def run_of(slot, r):
        return lax.rem(t + slot * (n_t // 2), n_t) * 2 + r

    out_copies = []
    for i in range(CHUNKS):
        rows = pl.ds(i * rows_c, rows_c)
        tc, gc = tcs[i], gcs[i]
        for copy in zi[2 * NF * i : 2 * NF * (i + 1)]:
            copy.wait_recv()

        def hidden(n):
            q, h = n // NH, lax.rem(n, NH)
            run, j = run_of(q, h // NF), lax.rem(h, NF)
            a0 = tc[q, table[0, 0, run, j]]
            a1 = tc[1 - q, table[0, 1, run, j]]
            v = dot(a0, w[q, 0, 2 * h]) + dot(a1, w[q, 0, 2 * h + 1])
            g0 = gc[q, table[1, 0, run, j]]
            g1 = gc[1 - q, table[1, 1, run, j]]
            d = dot_nt(g0, w[q, 1, 2 * h]) + dot_nt(g1, w[q, 1, 2 * h + 1])
            v2 = v * v
            th = jnp.tanh(ROOT * (v + CUBE * (v2 * v)))
            cdf = 0.5 * (1.0 + th)
            hv = (v * cdf).astype(BF16)
            slope = cdf + (0.5 * ROOT) * v * (1.0 - th * th) * (1.0 + (3.0 * CUBE) * v2)
            hid[q, h, rows] = hv
            hidt[q, h, :, rows] = hv.T
            dpre[q, h, rows] = (d * slope).astype(BF16)

        loop(2 * NH, hidden)

        for x in (1, 0):

            def outputs(f):
                acc = jnp.zeros((rows_c, B), F32)
                back = jnp.zeros((rows_c, B), F32)
                for s in range(2):
                    q = x if s == 0 else 1 - x
                    for r in range(2):
                        run = run_of(q, r)
                        h = r * NF + table[3, s, run, f]
                        acc += dot(hid[q, h, rows], w[q, 1, 2 * h + s])
                        h = r * NF + table[2, s, run, f]
                        back += dot_nt(dpre[q, h, rows], w[q, 0, 2 * h + s])
                obuf[x, 0, rows, lanes(f)] = acc.astype(BF16)
                obuf[x, 1, rows, lanes(f)] = back.astype(BF16)

            loop(NF, outputs)
            there = pl.ds(pl.multiple_of(keep_off + i * rows_c, rows_c), rows_c)
            for j, dst in enumerate((out_hbm, ig_hbm)):
                n = 2 * i + j
                if x == 1:
                    copy = remote(
                        obuf.at[1, j, rows], dst.at[there], zo_send.at[n], zo_recv.at[n], z_peer
                    )
                else:
                    copy = pltpu.make_async_copy(obuf.at[0, j, rows], dst.at[there], lo_sem.at[n])
                copy.start()
                out_copies.append(copy)

        def flip(n):
            x, f = n // NF, lax.rem(n, NF)
            tt[x, f, :, rows] = tc[x, f].T
            gj[x, f, rows] = gc[x, f]

        loop(2 * NF, flip)

    def exchange(q, n):
        return remote(snd.at[q, n], rcv.at[q, n], cs_send.at[q * 16 + n], cs_recv.at[q * 16 + n], sibling)

    def gradients(q):
        def block(h):
            run, j = run_of(q, h // NF), lax.rem(h, NF)

            def pair(s):
                x = q * (1 - s) + (1 - q) * s
                return (
                    dot(tt[x, table[0, s, run, j]], dpre[q, h]),
                    dot(hidt[q, h], gj[x, table[1, s, run, j]]),
                )

            gu, gd = pair(1 - core)
            snd[q, h] = gu.astype(BF16)
            snd[q, NH + h] = gd.astype(BF16)
            exchange(q, h).start()
            exchange(q, NH + h).start()
            gu, gd = pair(core)
            keep[q, h] = gu
            keep[q, NH + h] = gd

        loop(NH, block)

    def place(a, b):
        return pl.ds(pl.multiple_of(a * (64 - 48 * core) + b * (16 + 48 * core), 16), 16)

    def summed(q, a, b):
        return keep[q, :, place(a, b), :] + rcv[q, :, place(a, b), :].astype(F32)

    mine_1 = dp * (1 - core) + y * core
    mine_2 = y * (1 - core) + dp * core

    def stage_1(q):
        loop(2 * NH, lambda n: exchange(q, n).wait_recv())

        def part(n):
            a, b = n // n_y, lax.rem(n, n_y)
            s1[q, a, b] = summed(q, a, b).astype(BF16)

        loop(n_dp * n_y, part)
        for k in range(1, n_dp):
            stage_1_copy(q, k).start()

    def stage_1_copy(q, k):
        n = 3 * q + k - 1
        return remote(
            s1.at[q, lax.rem(mine_1 + k, n_dp)], r1.at[q, k - 1], r1_send.at[n], r1_recv.at[n], first_peer(k)
        )

    def stage_2(q):
        for k in range(1, n_dp):
            stage_1_copy(q, k).wait_recv()

        def part(b):
            v = summed(q, mine_1, b)
            for k in range(n_dp - 1):
                v = v + r1[q, k, b].astype(F32)
            f2[q, b] = v
            s2[q, b] = v.astype(BF16)

        loop(n_y, part)
        for k in range(1, n_y):
            stage_2_copy(q, k).start()

    def stage_2_copy(q, k):
        n = 3 * q + k - 1
        return remote(
            s2.at[q, lax.rem(mine_2 + k, n_y)], r2.at[q, k - 1], r2_send.at[n], r2_recv.at[n], second_peer(k)
        )

    def stage_3(q):
        for k in range(1, n_y):
            stage_2_copy(q, k).wait_recv()
        v = f2[q, mine_2]
        for k in range(n_y - 1):
            v = v + r2[q, k].astype(F32)
        return v

    gradients(1)
    stage_1(1)
    gradients(0)
    stage_1(0)
    stage_2(1)
    stage_2(0)
    zs[...] = stage_3(1).astype(BF16)
    z_return = remote(zs, zr, end_sem.at[0], end_sem.at[1], z_peer)
    z_return.start()
    f3[...] = stage_3(0)
    z_return.wait_recv()
    fx[...] = (f3[...] + zr[...].astype(F32)) * scale
    mine_8 = pl.ds(pl.multiple_of(core * 8, 8), 8)
    their_8 = pl.ds(pl.multiple_of((1 - core) * 8, 8), 8)
    last = remote(fx.at[:, their_8], fr, end_sem.at[2], end_sem.at[3], sibling)
    last.start()

    def write_mine(h):
        gup_ref[h, core] = fx[h, mine_8]
        gdn_ref[h, core] = fx[NH + h, mine_8]

    loop(NH, write_mine)
    last.wait_recv()

    def write_theirs(h):
        gup_ref[h, 1 - core] = fr[h]
        gdn_ref[h, 1 - core] = fr[NH + h]

    loop(NH, write_theirs)

    for copy in out_copies:
        copy.wait()
    for copy in zw + zi:
        copy.wait_send()
    for k in range(1, n_dp):
        first_copy(k, chip).wait_send()
    for m in range(n_dp):
        for k in range(1, n_y):
            second_copy(m, k, chip).wait_send()
    loop(n_dp * n_y, lambda u: sibling_copy(u).wait_send())
    for q in range(2):
        loop(2 * NH, functools.partial(lambda q, n: exchange(q, n).wait_send(), q))
        for k in range(1, n_dp):
            stage_1_copy(q, k).wait_send()
        for k in range(1, n_y):
            stage_2_copy(q, k).wait_send()
    z_return.wait_send()
    last.wait_send()


def on_device(tokens, out_grad, up_perm, down_perm, up_weight, down_weight):
    rows, width = tokens.shape
    n_dp, n_seq, n_t = (lax.axis_size(a) for a in ("dp", "seq", "tensor"))
    n_y = n_seq // 2
    half = rows // 2
    rows_c = half // CHUNKS
    units = 2 * NH
    scale = float(rows * n_dp * n_seq) ** (-0.5)
    upw = up_weight.reshape(units, B, B)
    dnw = down_weight.reshape(units, B, B)
    order = jnp.arange(NF, dtype=jnp.int32)
    held = [jnp.sum((p[..., None] == order) * order[:, None], axis=-2) for p in (up_perm, down_perm)]
    table = jnp.stack([up_perm, down_perm] + held).astype(jnp.int32)
    any_space = pl.BlockSpec(memory_space=pl.ANY)
    vmem = pl.BlockSpec(memory_space=pltpu.VMEM)
    smem = pl.BlockSpec(memory_space=pltpu.SMEM)
    dma = pltpu.SemaphoreType.DMA
    rows_chip = B // (n_dp * n_y)
    small = jax.ShapeDtypeStruct((NH, 2, rows_chip // 2, B), F32)
    return pl.pallas_call(
        functools.partial(kernel, (n_dp, n_seq, n_t), scale),
        out_shape=(
            jax.ShapeDtypeStruct((rows, width), BF16),
            jax.ShapeDtypeStruct((rows, width), BF16),
            small,
            small,
        ),
        in_specs=[smem, any_space, any_space, any_space, any_space],
        out_specs=(any_space, any_space, vmem, vmem),
        scratch_shapes=[
            pltpu.VMEM((2, 2, units, B, B), BF16),
            [pltpu.VMEM((2, NF, rows_c, B), BF16) for _ in range(CHUNKS)],
            [pltpu.VMEM((2, NF, rows_c, B), BF16) for _ in range(CHUNKS)],
            pltpu.VMEM((2, NF, B, half), BF16),
            pltpu.VMEM((2, NF, half, B), BF16),
            pltpu.VMEM((2, NH, half, B), BF16),
            pltpu.VMEM((2, NH, B, half), BF16),
            pltpu.VMEM((2, NH, half, B), BF16),
            pltpu.VMEM((2, 2, half, width), BF16),
            pltpu.VMEM((2, units, B, B), F32),
            pltpu.VMEM((2, units, B, B), BF16),
            pltpu.VMEM((2, units, B, B), BF16),
            pltpu.VMEM((2, n_dp, n_y, units, rows_chip, B), BF16),
            pltpu.VMEM((2, n_dp - 1, n_y, units, rows_chip, B), BF16),
            pltpu.VMEM((2, n_y, units, rows_chip, B), BF16),
            pltpu.VMEM((2, n_y, units, rows_chip, B), F32),
            pltpu.VMEM((2, n_y - 1, units, rows_chip, B), BF16),
            pltpu.VMEM((units, rows_chip, B), F32),
            pltpu.VMEM((units, rows_chip, B), BF16),
            pltpu.VMEM((units, rows_chip, B), BF16),
            pltpu.VMEM((units, rows_chip, B), F32),
            pltpu.VMEM((units, rows_chip // 2, B), F32),
            dma((2 + 2 * NF * CHUNKS,)),
            dma((4,)),
            dma((2 * NF * CHUNKS,)),
            dma((2 * NF * CHUNKS,)),
            dma((3 + 12,)),
            dma((16,)),
            dma((16,)),
            dma((16,)),
            dma((2 * CHUNKS,)),
            dma((2 * CHUNKS,)),
            dma((2 * CHUNKS,)),
            dma((32,)),
            dma((32,)),
            dma((6,)),
            dma((6,)),
            dma((6,)),
            dma((6,)),
            dma((4,)),
        ],
        compiler_params=pltpu.CompilerParams(
            collective_id=0, has_side_effects=True, vmem_limit_bytes=60 * 1024 * 1024
        ),
        name="butterfly",
    )(table, tokens, out_grad, upw, dnw)


def solution(mesh):
    in_specs = (
        P(("dp", "seq"), "tensor"),
        P(("dp", "seq"), "tensor"),
        P(),
        P(),
        P("tensor", None, None, None),
        P("tensor", None, None, None),
    )
    out_specs = (
        P(("dp", "seq"), "tensor"),
        P(("dp", "seq"), "tensor"),
        P("tensor", None, ("dp", "seq"), None),
        P("tensor", None, ("dp", "seq"), None),
    )
    return jax.shard_map(
        on_device, mesh=mesh, in_specs=in_specs, out_specs=out_specs, check_vma=False
    )
```

```python
import functools
import math

import jax
import jax.numpy as jnp
from jax import lax
from jax.experimental import pallas as pl
from jax.experimental.pallas import tpu as pltpu
from jax.sharding import PartitionSpec as P

F32 = jnp.float32
BF16 = jnp.bfloat16
B = 256
NF = 4
NH = 8
CHUNKS = 2
PIECES = 4
ROOT = math.sqrt(2.0 / math.pi)
CUBE = 0.044715


def dot(a, b):
    return jnp.dot(a, b, preferred_element_type=F32)


def dot_nt(a, b):
    return lax.dot_general(a, b, (((1,), (1,)), ((), ())), preferred_element_type=F32)


def lanes(block):
    return pl.ds(pl.multiple_of(block * B, B), B)


def loop(count, body):
    lax.fori_loop(0, count, lambda i, c: (body(i), c)[1], 0)


def kernel(
    sizes, scale,
    up_perm, down_perm, tok_hbm, grd_hbm, upw_hbm, dnw_hbm,
    out_hbm, ig_hbm, gup_ref, gdn_ref,
    w, tcs, gcs, tt, gj, hid, hidt, dpre, obuf,
    keep, snd, rcv, s1, r1, s2, f2, r2, f3, zs, zr, fx, fr, table,
    loc_sem, zw_sem, zi_send, zi_recv, ag_send, ag_recv, sb_send, sb_recv,
    zo_send, zo_recv, lo_sem, cs_send, cs_recv, r1_send, r1_recv, r2_send, r2_recv, end_sem,
):
    n_dp, n_seq, n_t = sizes
    n_y = n_seq // 2
    dp, seq, t = lax.axis_index("dp"), lax.axis_index("seq"), lax.axis_index("tensor")
    y, core = seq // 2, lax.rem(seq, 2)
    half = tok_hbm.shape[0] // 2
    rows_c = half // CHUNKS
    upper = t // (n_t // 2)
    keep_off = upper * half
    send_off = half - keep_off

    def peer(d, s, q):
        return {"dp": d, "seq": s, "tensor": q}

    z_peer = peer(dp, seq, lax.rem(t + n_t // 2, n_t))
    sibling = peer(dp, seq + 1 - 2 * core, t)

    def first_peer(k):
        return peer(lax.rem(dp + k * (1 - core), n_dp), lax.rem(seq + 2 * k * core, n_seq), t)

    def second_peer(k):
        return peer(lax.rem(dp + k * core, n_dp), lax.rem(seq + 2 * k * (1 - core), n_seq), t)

    def remote(src, dst, send, recv, device):
        return pltpu.make_async_remote_copy(
            src_ref=src, dst_ref=dst, send_sem=send, recv_sem=recv,
            device_id=device, device_id_type=pl.DeviceIdType.MESH,
        )

    local = [
        pltpu.make_async_copy(upw_hbm, w.at[0, 0], loc_sem.at[0]),
        pltpu.make_async_copy(dnw_hbm, w.at[0, 1], loc_sem.at[1]),
    ]
    for i in range(CHUNKS):
        rows = pl.ds(pl.multiple_of(keep_off + i * rows_c, rows_c), rows_c)
        for j, (src, dst) in enumerate(((tok_hbm, tcs[i]), (grd_hbm, gcs[i]))):
            for f in range(NF):
                n = (2 * i + j) * NF + f
                local.append(
                    pltpu.make_async_copy(src.at[rows, f * B : (f + 1) * B], dst.at[0, f], loc_sem.at[2 + n])
                )
    for copy in local:
        copy.start()

    barrier = pltpu.get_barrier_semaphore()
    greeted = [z_peer, sibling]
    greeted += [first_peer(k) for k in range(1, n_dp)] + [second_peer(k) for k in range(1, n_y)]
    for device in greeted:
        pl.semaphore_signal(barrier, inc=1, device_id=device, device_id_type=pl.DeviceIdType.MESH)
    pl.semaphore_wait(barrier, len(greeted))

    chip = dp * n_y + y
    hrows = pl.ds(pl.multiple_of(core * (B // 2), B // 2), B // 2)

    def unit(u, part=hrows):
        return w.at[1, :, u, part]

    zw = [
        remote(upw_hbm.at[chip, hrows], w.at[1, 0, chip, hrows], zw_sem.at[0], zw_sem.at[1], z_peer),
        remote(dnw_hbm.at[chip, hrows], w.at[1, 1, chip, hrows], zw_sem.at[2], zw_sem.at[3], z_peer),
    ]
    for copy in zw:
        copy.start()
    zi = []
    for i in range(CHUNKS):
        rows = pl.ds(pl.multiple_of(send_off + i * rows_c, rows_c), rows_c)
        for j, (src, dst) in enumerate(((tok_hbm, tcs[i]), (grd_hbm, gcs[i]))):
            for f in range(NF):
                n = (2 * i + j) * NF + f
                zi.append(
                    remote(
                        src.at[rows, f * B : (f + 1) * B], dst.at[1, f], zi_send.at[n], zi_recv.at[n], z_peer
                    )
                )
                zi[-1].start()

    def first_copy(k, u):
        return remote(unit(u), unit(u), ag_send.at[k - 1], ag_recv.at[u], first_peer(k))

    def second_copy(m, k, u):
        return remote(unit(u), unit(u), ag_send.at[3 + 3 * m + k - 1], ag_recv.at[u], second_peer(k))

    def sibling_copy(u):
        return remote(unit(u), unit(u), sb_send.at[u], sb_recv.at[u], sibling)

    other = pl.ds(pl.multiple_of((1 - core) * (B // 2), B // 2), B // 2)

    def sibling_arrival(u):
        return remote(unit(u, other), unit(u, other), sb_send.at[u], sb_recv.at[u], sibling)

    def moved(u_dp, u_y, k1, k2):
        a = lax.rem(u_dp + 8 * n_dp - k1 * (1 - core) - k2 * core, n_dp)
        b = lax.rem(u_y + 8 * n_y - k1 * core - k2 * (1 - core), n_y)
        return a * n_y + b

    def fill(n):
        s, run = n // 4, lax.rem(n, 4)
        source = lax.rem(t + (run // 2) * (n_t // 2), n_t) * 2 + lax.rem(run, 2)
        for p, perm in enumerate((up_perm, down_perm)):
            code = jnp.int32(0)
            for j in range(NF):
                block = perm[s, j, source]
                table[(p * 2 + s) * 16 + run * NF + j] = block
                high = lax.div(block, jnp.int32(2))
                low = block - 2 * high
                code = code + j * ((1 + 3 * low) * (1 + 15 * high))
            for f in range(NF):
                table[64 + (p * 2 + s) * 16 + run * NF + f] = lax.rem(lax.div(code, jnp.int32(4**f)), jnp.int32(4))

    loop(8, fill)

    def entry(kind, s, run, n):
        return table[(kind * 2 + s) * 16 + run * NF + n]

    for copy in zw:
        copy.wait_recv()
    for k in range(1, n_dp):
        first_copy(k, chip).start()
    for m in range(n_dp):
        u = moved(dp, y, m, 0)
        if m:
            first_copy(m, u).wait_recv()
        for k in range(1, n_y):
            second_copy(m, k, u).start()
        sibling_copy(u).start()
    for k in range(1, n_y):
        for m in range(n_dp):
            u = moved(dp, y, m, k)
            second_copy(m, k, u).wait_recv()
            sibling_copy(u).start()
    for copy in local:
        copy.wait()
    loop(n_dp * n_y, lambda u: sibling_arrival(u).wait_recv())

    out_copies = []

    def forward(i):
        rows = pl.ds(i * rows_c, rows_c)
        tc, gc = tcs[i], gcs[i]
        for copy in zi[2 * NF * i : 2 * NF * (i + 1)]:
            copy.wait_recv()

        def hidden(n):
            q, h = n // NH, lax.rem(n, NH)
            run, j = n // NF, lax.rem(n, NF)
            a0 = tc[q, entry(0, 0, run, j)]
            a1 = tc[1 - q, entry(0, 1, run, j)]
            v = dot(a0, w[q, 0, 2 * h]) + dot(a1, w[q, 0, 2 * h + 1])
            g0 = gc[q, entry(1, 0, run, j)]
            g1 = gc[1 - q, entry(1, 1, run, j)]
            d = dot_nt(g0, w[q, 1, 2 * h]) + dot_nt(g1, w[q, 1, 2 * h + 1])
            v2 = v * v
            th = jnp.tanh(ROOT * (v + CUBE * (v2 * v)))
            cdf = 0.5 * (1.0 + th)
            hv = (v * cdf).astype(BF16)
            slope = cdf + (0.5 * ROOT) * v * (1.0 - th * th) * (1.0 + (3.0 * CUBE) * v2)
            hid[q, h, rows] = hv
            hidt[q, h, :, rows] = hv.T
            dpre[q, h, rows] = (d * slope).astype(BF16)

        loop(2 * NH, hidden)

        def flip(n):
            x, f = n // NF, lax.rem(n, NF)
            tt[x, f, :, rows] = tc[x, f].T
            gj[x, f, rows] = gc[x, f]

        loop(2 * NF, flip)

    def outputs(i, x):
        rows = pl.ds(i * rows_c, rows_c)

        def block(f):
            acc = jnp.zeros((rows_c, B), F32)
            back = jnp.zeros((rows_c, B), F32)
            for s in range(2):
                q = x if s == 0 else 1 - x
                for r in range(2):
                    h = r * NF + entry(3, s, 2 * q + r, f)
                    acc += dot(hid[q, h, rows], w[q, 1, 2 * h + s])
                    h = r * NF + entry(2, s, 2 * q + r, f)
                    back += dot_nt(dpre[q, h, rows], w[q, 0, 2 * h + s])
            obuf[x, 0, rows, lanes(f)] = acc.astype(BF16)
            obuf[x, 1, rows, lanes(f)] = back.astype(BF16)

        loop(NF, block)
        there = pl.ds(pl.multiple_of(keep_off + i * rows_c, rows_c), rows_c)
        for j, dst in enumerate((out_hbm, ig_hbm)):
            n = 2 * i + j
            if x == 1:
                copy = remote(
                    obuf.at[1, j, rows], dst.at[there], zo_send.at[n], zo_recv.at[n], z_peer
                )
            else:
                copy = pltpu.make_async_copy(obuf.at[0, j, rows], dst.at[there], lo_sem.at[n])
            copy.start()
            out_copies.append(copy)

    def exchange(q, n):
        return remote(snd.at[q, n], rcv.at[q, n], cs_send.at[q * 16 + n], cs_recv.at[q * 16 + n], sibling)

    def gradients(q):
        def block(h):
            run, j = 2 * q + h // NF, lax.rem(h, NF)

            def pair(s):
                x = q * (1 - s) + (1 - q) * s
                return (
                    dot(tt[x, entry(0, s, run, j)], dpre[q, h]),
                    dot(hidt[q, h], gj[x, entry(1, s, run, j)]),
                )

            gu, gd = pair(1 - core)
            snd[q, h] = gu.astype(BF16)
            snd[q, NH + h] = gd.astype(BF16)
            exchange(q, h).start()
            exchange(q, NH + h).start()
            gu, gd = pair(core)
            keep[q, h] = gu
            keep[q, NH + h] = gd

        loop(NH, block)

    def place(a, b):
        return pl.ds(pl.multiple_of(a * (64 - 48 * core) + b * (16 + 48 * core), 16), 16)

    def summed(q, a, b):
        return keep[q, :, place(a, b), :] + rcv[q, :, place(a, b), :].astype(F32)

    mine_1 = dp * (1 - core) + y * core
    mine_2 = y * (1 - core) + dp * core

    def stage_1(q):
        loop(2 * NH, lambda n: exchange(q, n).wait_recv())

        def part(n):
            a, b = n // n_y, lax.rem(n, n_y)
            s1[q, a, b] = summed(q, a, b).astype(BF16)

        loop(n_dp * n_y, part)
        for k in range(1, n_dp):
            stage_1_copy(q, k).start()

    def stage_1_copy(q, k):
        n = 3 * q + k - 1
        return remote(
            s1.at[q, lax.rem(mine_1 + k, n_dp)], r1.at[q, k - 1], r1_send.at[n], r1_recv.at[n], first_peer(k)
        )

    def stage_2(q):
        for k in range(1, n_dp):
            stage_1_copy(q, k).wait_recv()

        def part(b):
            v = summed(q, mine_1, b)
            for k in range(n_dp - 1):
                v = v + r1[q, k, b].astype(F32)
            f2[q, b] = v
            s2[q, b] = v.astype(BF16)

        loop(n_y, part)
        for k in range(1, n_y):
            stage_2_copy(q, k).start()

    def stage_2_copy(q, k):
        n = 3 * q + k - 1
        return remote(
            s2.at[q, lax.rem(mine_2 + k, n_y)], r2.at[q, k - 1], r2_send.at[n], r2_recv.at[n], second_peer(k)
        )

    def stage_3(q):
        for k in range(1, n_y):
            stage_2_copy(q, k).wait_recv()
        v = f2[q, mine_2]
        for k in range(n_y - 1):
            v = v + r2[q, k].astype(F32)
        return v

    for i in range(CHUNKS):
        forward(i)
        if i < CHUNKS - 1:
            outputs(i, 1)
            outputs(i, 0)
    gradients(1)
    stage_1(1)
    gradients(0)
    stage_1(0)
    outputs(CHUNKS - 1, 1)
    stage_2(1)
    outputs(CHUNKS - 1, 0)
    stage_2(0)
    zs[...] = stage_3(1).astype(BF16)
    z_return = remote(zs, zr, end_sem.at[0], end_sem.at[1], z_peer)
    z_return.start()
    f3[...] = stage_3(0)
    z_return.wait_recv()
    fx[...] = (f3[...] + zr[...].astype(F32)) * scale
    mine_8 = pl.ds(pl.multiple_of(core * 8, 8), 8)
    their_8 = pl.ds(pl.multiple_of((1 - core) * 8, 8), 8)
    last = remote(fx.at[:, their_8], fr, end_sem.at[2], end_sem.at[3], sibling)
    last.start()

    def write_mine(h):
        gup_ref[h, core] = fx[h, mine_8]
        gdn_ref[h, core] = fx[NH + h, mine_8]

    loop(NH, write_mine)
    last.wait_recv()

    def write_theirs(h):
        gup_ref[h, 1 - core] = fr[h]
        gdn_ref[h, 1 - core] = fr[NH + h]

    loop(NH, write_theirs)

    for copy in out_copies:
        copy.wait()
    for copy in zw + zi:
        copy.wait_send()
    for k in range(1, n_dp):
        first_copy(k, chip).wait_send()
    for m in range(n_dp):
        for k in range(1, n_y):
            second_copy(m, k, chip).wait_send()
    loop(n_dp * n_y, lambda u: sibling_copy(u).wait_send())
    for q in range(2):
        loop(2 * NH, functools.partial(lambda q, n: exchange(q, n).wait_send(), q))
        for k in range(1, n_dp):
            stage_1_copy(q, k).wait_send()
        for k in range(1, n_y):
            stage_2_copy(q, k).wait_send()
    z_return.wait_send()
    last.wait_send()


def hand_over(*refs):
    sources, targets, buffers, sem = refs[:4], refs[4:8], refs[8:12], refs[12]
    copies = []
    for i in range(4):
        step = sources[i].shape[0] // PIECES
        for p in range(PIECES):
            part = pl.ds(p * step, step)
            copies.append(
                [
                    pltpu.make_async_copy(sources[i].at[part], buffers[i].at[part], sem.at[i, p, 0]),
                    pltpu.make_async_copy(buffers[i].at[part], targets[i].at[part], sem.at[i, p, 1]),
                ]
            )
            copies[-1][0].start()
    for arrive, leave in copies:
        arrive.wait()
        leave.start()
    for _, leave in copies:
        leave.wait()


def on_device(tokens, out_grad, up_perm, down_perm, up_weight, down_weight):
    rows, width = tokens.shape
    n_dp, n_seq, n_t = (lax.axis_size(a) for a in ("dp", "seq", "tensor"))
    n_y = n_seq // 2
    half = rows // 2
    rows_c = half // CHUNKS
    units = 2 * NH
    scale = float(rows * n_dp * n_seq) ** (-0.5)
    upw = up_weight.reshape(units, B, B)
    dnw = down_weight.reshape(units, B, B)
    any_space = pl.BlockSpec(memory_space=pl.ANY)
    vmem = pl.BlockSpec(memory_space=pltpu.VMEM)
    smem = pl.BlockSpec(memory_space=pltpu.SMEM)
    dma = pltpu.SemaphoreType.DMA
    rows_chip = B // (n_dp * n_y)
    small = jax.ShapeDtypeStruct((NH, 2, rows_chip // 2, B), F32)
    results = pl.pallas_call(
        functools.partial(kernel, (n_dp, n_seq, n_t), scale),
        out_shape=(
            jax.ShapeDtypeStruct((rows, width), BF16),
            jax.ShapeDtypeStruct((rows, width), BF16),
            small,
            small,
        ),
        in_specs=[smem, smem, any_space, any_space, any_space, any_space],
        out_specs=(any_space, any_space, vmem, vmem),
        scratch_shapes=[
            pltpu.VMEM((2, 2, units, B, B), BF16),
            [pltpu.VMEM((2, NF, rows_c, B), BF16) for _ in range(CHUNKS)],
            [pltpu.VMEM((2, NF, rows_c, B), BF16) for _ in range(CHUNKS)],
            pltpu.VMEM((2, NF, B, half), BF16),
            pltpu.VMEM((2, NF, half, B), BF16),
            pltpu.VMEM((2, NH, half, B), BF16),
            pltpu.VMEM((2, NH, B, half), BF16),
            pltpu.VMEM((2, NH, half, B), BF16),
            pltpu.VMEM((2, 2, half, width), BF16),
            pltpu.VMEM((2, units, B, B), F32),
            pltpu.VMEM((2, units, B, B), BF16),
            pltpu.VMEM((2, units, B, B), BF16),
            pltpu.VMEM((2, n_dp, n_y, units, rows_chip, B), BF16),
            pltpu.VMEM((2, n_dp - 1, n_y, units, rows_chip, B), BF16),
            pltpu.VMEM((2, n_y, units, rows_chip, B), BF16),
            pltpu.VMEM((2, n_y, units, rows_chip, B), F32),
            pltpu.VMEM((2, n_y - 1, units, rows_chip, B), BF16),
            pltpu.VMEM((units, rows_chip, B), F32),
            pltpu.VMEM((units, rows_chip, B), BF16),
            pltpu.VMEM((units, rows_chip, B), BF16),
            pltpu.VMEM((units, rows_chip, B), F32),
            pltpu.VMEM((units, rows_chip // 2, B), F32),
            pltpu.SMEM((128,), jnp.int32),
            dma((2 + 2 * NF * CHUNKS,)),
            dma((4,)),
            dma((2 * NF * CHUNKS,)),
            dma((2 * NF * CHUNKS,)),
            dma((3 + 12,)),
            dma((16,)),
            dma((16,)),
            dma((16,)),
            dma((2 * CHUNKS,)),
            dma((2 * CHUNKS,)),
            dma((2 * CHUNKS,)),
            dma((32,)),
            dma((32,)),
            dma((6,)),
            dma((6,)),
            dma((6,)),
            dma((6,)),
            dma((4,)),
        ],
        compiler_params=pltpu.CompilerParams(
            collective_id=0, has_side_effects=True, vmem_limit_bytes=60 * 1024 * 1024
        ),
        name="butterfly",
    )(jnp.swapaxes(up_perm, 1, 2), jnp.swapaxes(down_perm, 1, 2), tokens, out_grad, upw, dnw)
    return pl.pallas_call(
        hand_over,
        out_shape=tuple(jax.ShapeDtypeStruct(r.shape, r.dtype) for r in results),
        in_specs=[any_space] * 4,
        out_specs=(any_space,) * 4,
        scratch_shapes=[pltpu.VMEM(r.shape, r.dtype) for r in results] + [dma((4, PIECES, 2))],
        name="results",
    )(*results)


def solution(mesh):
    in_specs = (
        P(("dp", "seq"), "tensor"),
        P(("dp", "seq"), "tensor"),
        P(),
        P(),
        P("tensor", None, None, None),
        P("tensor", None, None, None),
    )
    out_specs = (
        P(("dp", "seq"), "tensor"),
        P(("dp", "seq"), "tensor"),
        P("tensor", None, ("dp", "seq"), None),
        P("tensor", None, ("dp", "seq"), None),
    )
    return jax.shard_map(
        on_device, mesh=mesh, in_specs=in_specs, out_specs=out_specs, check_vma=False
    )
```

```python
import functools
import math

import jax
import jax.numpy as jnp
from jax import lax
from jax.experimental import pallas as pl
from jax.experimental.pallas import tpu as pltpu
from jax.sharding import PartitionSpec as P

F32 = jnp.float32
BF16 = jnp.bfloat16
B = 256
NF = 4
NH = 8
SPLIT = (96, 96, 64)
CHUNKS = len(SPLIT)
PIECES = 4
ROOT = math.sqrt(2.0 / math.pi)
CUBE = 0.044715


def dot(a, b):
    return jnp.dot(a, b, preferred_element_type=F32)


def dot_nt(a, b):
    return lax.dot_general(a, b, (((1,), (1,)), ((), ())), preferred_element_type=F32)


def lanes(block):
    return pl.ds(pl.multiple_of(block * B, B), B)


def loop(count, body):
    lax.fori_loop(0, count, lambda i, c: (body(i), c)[1], 0)


def kernel(
    sizes, scale,
    up_perm, down_perm, tok_hbm, grd_hbm, upw_hbm, dnw_hbm,
    out_hbm, ig_hbm, gup_ref, gdn_ref,
    w, tcs, gcs, tj, tt, gj, hid, dpre, obuf,
    keep, snd, rcv, s1, rf, rn, cb, rb, s2, f2, r2, f3, zs, zr, fx, fr, table,
    loc_sem, zw_sem, zi_send, zi_recv, ag_send, ag_recv, sb_send, sb_recv,
    zo_send, zo_recv, lo_sem, cs_send, cs_recv, r1_send, r1_recv, r2_send, r2_recv, end_sem,
):
    n_dp, n_seq, n_t = sizes
    n_y = n_seq // 2
    dp, seq, t = lax.axis_index("dp"), lax.axis_index("seq"), lax.axis_index("tensor")
    y, core = seq // 2, lax.rem(seq, 2)
    half = tok_hbm.shape[0] // 2
    upper = t // (n_t // 2)
    keep_off = upper * half
    send_off = half - keep_off

    def chunk(i, offset=0):
        start = sum(SPLIT[:i])
        if isinstance(offset, int):
            return pl.ds(start, SPLIT[i])
        return pl.ds(pl.multiple_of(offset + start, 32), SPLIT[i])

    def peer(d, s, q):
        return {"dp": d, "seq": s, "tensor": q}

    z_peer = peer(dp, seq, lax.rem(t + n_t // 2, n_t))
    sibling = peer(dp, seq + 1 - 2 * core, t)

    def first_peer(k):
        return peer(lax.rem(dp + k * (1 - core), n_dp), lax.rem(seq + 2 * k * core, n_seq), t)

    def second_peer(k):
        return peer(lax.rem(dp + k * core, n_dp), lax.rem(seq + 2 * k * (1 - core), n_seq), t)

    def remote(src, dst, send, recv, device):
        return pltpu.make_async_remote_copy(
            src_ref=src, dst_ref=dst, send_sem=send, recv_sem=recv,
            device_id=device, device_id_type=pl.DeviceIdType.MESH,
        )

    local = [
        pltpu.make_async_copy(upw_hbm, w.at[0, 0], loc_sem.at[0]),
        pltpu.make_async_copy(dnw_hbm, w.at[0, 1], loc_sem.at[1]),
    ]
    for i in range(CHUNKS):
        rows = chunk(i, keep_off)
        for j, (src, dst) in enumerate(((tok_hbm, tcs[i]), (grd_hbm, gcs[i]))):
            for f in range(NF):
                n = (2 * i + j) * NF + f
                local.append(
                    pltpu.make_async_copy(src.at[rows, f * B : (f + 1) * B], dst.at[0, f], loc_sem.at[2 + n])
                )
    for copy in local:
        copy.start()

    barrier = pltpu.get_barrier_semaphore()
    greeted = [z_peer, sibling]
    greeted += [first_peer(k) for k in range(1, n_dp)] + [second_peer(k) for k in range(1, n_y)]
    for device in greeted:
        pl.semaphore_signal(barrier, inc=1, device_id=device, device_id_type=pl.DeviceIdType.MESH)
    pl.semaphore_wait(barrier, len(greeted))

    chip = dp * n_y + y
    hrows = pl.ds(pl.multiple_of(core * (B // 2), B // 2), B // 2)

    def unit(u, part=hrows):
        return w.at[1, :, u, part]

    zw = [
        remote(upw_hbm.at[chip, hrows], w.at[1, 0, chip, hrows], zw_sem.at[0], zw_sem.at[1], z_peer),
        remote(dnw_hbm.at[chip, hrows], w.at[1, 1, chip, hrows], zw_sem.at[2], zw_sem.at[3], z_peer),
    ]
    for copy in zw:
        copy.start()
    zi = []
    for i in range(CHUNKS):
        rows = chunk(i, send_off)
        for j, (src, dst) in enumerate(((tok_hbm, tcs[i]), (grd_hbm, gcs[i]))):
            for f in range(NF):
                n = (2 * i + j) * NF + f
                zi.append(
                    remote(
                        src.at[rows, f * B : (f + 1) * B], dst.at[1, f], zi_send.at[n], zi_recv.at[n], z_peer
                    )
                )
                zi[-1].start()

    def first_copy(k, u):
        return remote(unit(u), unit(u), ag_send.at[k - 1], ag_recv.at[u], first_peer(k))

    def second_copy(m, k, u):
        return remote(unit(u), unit(u), ag_send.at[3 + 3 * m + k - 1], ag_recv.at[u], second_peer(k))

    def sibling_copy(u):
        return remote(unit(u), unit(u), sb_send.at[u], sb_recv.at[u], sibling)

    other = pl.ds(pl.multiple_of((1 - core) * (B // 2), B // 2), B // 2)

    def sibling_arrival(u):
        return remote(unit(u, other), unit(u, other), sb_send.at[u], sb_recv.at[u], sibling)

    def moved(u_dp, u_y, k1, k2):
        a = lax.rem(u_dp + 8 * n_dp - k1 * (1 - core) - k2 * core, n_dp)
        b = lax.rem(u_y + 8 * n_y - k1 * core - k2 * (1 - core), n_y)
        return a * n_y + b

    def fill(n):
        s, run = n // 4, lax.rem(n, 4)
        source = lax.rem(t + (run // 2) * (n_t // 2), n_t) * 2 + lax.rem(run, 2)
        for p, perm in enumerate((up_perm, down_perm)):
            code = jnp.int32(0)
            for j in range(NF):
                block = perm[s, j, source]
                table[(p * 2 + s) * 16 + run * NF + j] = block
                high = lax.div(block, jnp.int32(2))
                low = block - 2 * high
                code = code + j * ((1 + 3 * low) * (1 + 15 * high))
            for f in range(NF):
                table[64 + (p * 2 + s) * 16 + run * NF + f] = lax.rem(lax.div(code, jnp.int32(4**f)), jnp.int32(4))

    loop(8, fill)

    def entry(kind, s, run, n):
        return table[(kind * 2 + s) * 16 + run * NF + n]

    for copy in zw:
        copy.wait_recv()
    for k in range(1, n_dp):
        first_copy(k, chip).start()
    for m in range(n_dp):
        u = moved(dp, y, m, 0)
        if m:
            first_copy(m, u).wait_recv()
        for k in range(1, n_y):
            second_copy(m, k, u).start()
        sibling_copy(u).start()
    for k in range(1, n_y):
        for m in range(n_dp):
            u = moved(dp, y, m, k)
            second_copy(m, k, u).wait_recv()
            sibling_copy(u).start()
    for copy in local:
        copy.wait()
    loop(n_dp * n_y, lambda u: sibling_arrival(u).wait_recv())

    out_copies = []

    def forward(i):
        rows = chunk(i)
        tc, gc = tcs[i], gcs[i]
        for copy in zi[2 * NF * i : 2 * NF * (i + 1)]:
            copy.wait_recv()

        def hidden(n):
            q, h = n // NH, lax.rem(n, NH)
            run, j = n // NF, lax.rem(n, NF)
            a0 = tc[q, entry(0, 0, run, j)]
            a1 = tc[1 - q, entry(0, 1, run, j)]
            v = dot(a0, w[q, 0, 2 * h]) + dot(a1, w[q, 0, 2 * h + 1])
            g0 = gc[q, entry(1, 0, run, j)]
            g1 = gc[1 - q, entry(1, 1, run, j)]
            d = dot_nt(g0, w[q, 1, 2 * h]) + dot_nt(g1, w[q, 1, 2 * h + 1])
            v2 = v * v
            th = jnp.tanh(ROOT * (v + CUBE * (v2 * v)))
            cdf = 0.5 * (1.0 + th)
            hv = (v * cdf).astype(BF16)
            slope = cdf + (0.5 * ROOT) * v * (1.0 - th * th) * (1.0 + (3.0 * CUBE) * v2)
            hid[q, h, rows] = hv
            dpre[q, h, rows] = (d * slope).astype(BF16)

        loop(2 * NH, hidden)

        def join(n):
            x, f = n // NF, lax.rem(n, NF)
            tj[x, f, rows] = tc[x, f]
            gj[x, f, rows] = gc[x, f]

        loop(2 * NF, join)

    def outputs(i, x):
        rows = chunk(i)

        def block(f):
            acc = jnp.zeros((SPLIT[i], B), F32)
            back = jnp.zeros((SPLIT[i], B), F32)
            for s in range(2):
                q = x if s == 0 else 1 - x
                for r in range(2):
                    h = r * NF + entry(3, s, 2 * q + r, f)
                    acc += dot(hid[q, h, rows], w[q, 1, 2 * h + s])
                    h = r * NF + entry(2, s, 2 * q + r, f)
                    back += dot_nt(dpre[q, h, rows], w[q, 0, 2 * h + s])
            obuf[x, 0, rows, lanes(f)] = acc.astype(BF16)
            obuf[x, 1, rows, lanes(f)] = back.astype(BF16)

        loop(NF, block)
        there = chunk(i, keep_off)
        for j, dst in enumerate((out_hbm, ig_hbm)):
            n = 2 * i + j
            if x == 1:
                copy = remote(
                    obuf.at[1, j, rows], dst.at[there], zo_send.at[n], zo_recv.at[n], z_peer
                )
            else:
                copy = pltpu.make_async_copy(obuf.at[0, j, rows], dst.at[there], lo_sem.at[n])
            copy.start()
            out_copies.append(copy)

    def exchange(i, n):
        return remote(snd.at[i, n], rcv.at[i, n], cs_send.at[8 * i + n], cs_recv.at[8 * i + n], sibling)

    def gradients(i):
        q, r = 1 - i // 2, i % 2
        run = 2 * q + r

        def block(j):
            h = r * NF + j
            hidden_t = hid[q, h].T

            def pair(s):
                x = q * (1 - s) + (1 - q) * s
                return (
                    dot(tt[x, entry(0, s, run, j)], dpre[q, h]),
                    dot(hidden_t, gj[x, entry(1, s, run, j)]),
                )

            gu, gd = pair(1 - core)
            snd[i, j] = gu.astype(BF16)
            snd[i, NF + j] = gd.astype(BF16)
            exchange(i, j).start()
            exchange(i, NF + j).start()
            gu, gd = pair(core)
            keep[i, j] = gu
            keep[i, NF + j] = gd

        loop(NF, block)

    def place(a, b):
        return pl.ds(pl.multiple_of(a * (64 - 48 * core) + b * (16 + 48 * core), 16), 16)

    def summed(i, a, b):
        return keep[i, :, place(a, b), :] + rcv[i, :, place(a, b), :].astype(F32)

    mine_1 = dp * (1 - core) + y * core
    mine_2 = y * (1 - core) + dp * core
    down_1, up_1, far_1 = (lax.rem(mine_1 + k, n_dp) for k in (3, 1, 2))
    halves = pl.ds(0, 2), pl.ds(2, 2)

    def far_copy(i, d):
        return remote(
            s1.at[i, far_1, halves[d]], rf.at[i, d], r1_send.at[0, i, d], r1_recv.at[0, i, d], first_peer(3 - 2 * d)
        )

    def near_copy(i, d):
        return remote(
            s1.at[i, up_1 if d else down_1, halves[1 - d]], rn.at[i, d],
            r1_send.at[1, i, d], r1_recv.at[1, i, d], first_peer(3 - 2 * d),
        )

    def both_copy(i, d):
        return remote(
            cb.at[i, d], rb.at[i, d], r1_send.at[2, i, d], r1_recv.at[2, i, d], first_peer(3 - 2 * d)
        )

    def stage_1(i):
        loop(2 * NF, lambda n: exchange(i, n).wait_recv())

        def part(n):
            a, b = n // n_y, lax.rem(n, n_y)
            s1[i, a, b] = summed(i, a, b).astype(BF16)

        loop(n_dp * n_y, part)
        for d in range(2):
            far_copy(i, d).start()
        for d in range(2):
            near_copy(i, d).start()

    def stage_2(i):
        for d in range(2):
            far_copy(i, d).wait_recv()

            def part(b):
                v = summed(i, up_1 if d else down_1, 2 * d + b) + rf[i, d, b].astype(F32)
                cb[i, d, b] = v.astype(BF16)

            loop(2, part)
            both_copy(i, d).start()

    def stage_3(i):
        for d in range(2):
            near_copy(i, d).wait_recv()
        for d in range(2):
            both_copy(i, d).wait_recv()
        for d in range(2):

            def part(b):
                v = summed(i, mine_1, 2 * d + b) + rb[i, d, b].astype(F32) + rn[i, 1 - d, b].astype(F32)
                f2[i, 2 * d + b] = v
                s2[i, 2 * d + b] = v.astype(BF16)

            loop(2, part)
        for k in range(1, n_y):
            second_axis_copy(i, k).start()

    def second_axis_copy(i, k):
        n = 3 * i + k - 1
        return remote(
            s2.at[i, lax.rem(mine_2 + k, n_y)], r2.at[i, k - 1], r2_send.at[n], r2_recv.at[n], second_peer(k)
        )

    def stage_4(i):
        for k in range(1, n_y):
            second_axis_copy(i, k).wait_recv()
        v = f2[i, mine_2]
        for k in range(n_y - 1):
            v = v + r2[i, k].astype(F32)
        return v

    def return_copy(i):
        return remote(zs.at[i], zr.at[i], end_sem.at[0, i], end_sem.at[1, i], z_peer)

    for i in range(CHUNKS):
        forward(i)
        if i < CHUNKS - 1:
            outputs(i, 1)
            outputs(i, 0)

    def flip(n):
        x, f = n // NF, lax.rem(n, NF)
        tt[x, f] = tj[x, f].T

    loop(2 * NF, flip)
    for i in range(4):
        gradients(i)
        stage_1(i)
        if i:
            stage_2(i - 1)
    outputs(CHUNKS - 1, 1)
    stage_2(3)
    stage_3(0)
    stage_3(1)
    for i in range(2):
        zs[i] = stage_4(i).astype(BF16)
        return_copy(i).start()
    outputs(CHUNKS - 1, 0)
    stage_3(2)
    stage_3(3)
    for i in range(2):
        f3[i] = stage_4(2 + i)
    for i in range(2):
        return_copy(i).wait_recv()
        fx[i] = (f3[i] + zr[i].astype(F32)) * scale
    mine_8 = pl.ds(pl.multiple_of(core * 8, 8), 8)
    their_8 = pl.ds(pl.multiple_of((1 - core) * 8, 8), 8)
    last = remote(fx.at[:, :, their_8], fr, end_sem.at[0, 2], end_sem.at[1, 2], sibling)
    last.start()

    def write_mine(h):
        r, j = h // NF, lax.rem(h, NF)
        gup_ref[h, core] = fx[r, j, mine_8]
        gdn_ref[h, core] = fx[r, NF + j, mine_8]

    loop(NH, write_mine)
    last.wait_recv()

    def write_theirs(h):
        r, j = h // NF, lax.rem(h, NF)
        gup_ref[h, 1 - core] = fr[r, j]
        gdn_ref[h, 1 - core] = fr[r, NF + j]

    loop(NH, write_theirs)

    for copy in out_copies:
        copy.wait()
    for copy in zw + zi:
        copy.wait_send()
    for k in range(1, n_dp):
        first_copy(k, chip).wait_send()
    for m in range(n_dp):
        for k in range(1, n_y):
            second_copy(m, k, chip).wait_send()
    loop(n_dp * n_y, lambda u: sibling_copy(u).wait_send())
    for i in range(4):
        loop(2 * NF, functools.partial(lambda i, n: exchange(i, n).wait_send(), i))
        for d in range(2):
            far_copy(i, d).wait_send()
            near_copy(i, d).wait_send()
            both_copy(i, d).wait_send()
        for k in range(1, n_y):
            second_axis_copy(i, k).wait_send()
    for i in range(2):
        return_copy(i).wait_send()
    last.wait_send()


def hand_over(*refs):
    sources, targets, buffers, sem = refs[:4], refs[4:8], refs[8:12], refs[12]
    copies = []
    for i in range(4):
        step = sources[i].shape[0] // PIECES
        for p in range(PIECES):
            part = pl.ds(p * step, step)
            copies.append(
                [
                    pltpu.make_async_copy(sources[i].at[part], buffers[i].at[part], sem.at[i, p, 0]),
                    pltpu.make_async_copy(buffers[i].at[part], targets[i].at[part], sem.at[i, p, 1]),
                ]
            )
            copies[-1][0].start()
    for arrive, leave in copies:
        arrive.wait()
        leave.start()
    for _, leave in copies:
        leave.wait()


def on_device(tokens, out_grad, up_perm, down_perm, up_weight, down_weight):
    rows, width = tokens.shape
    n_dp, n_seq, n_t = (lax.axis_size(a) for a in ("dp", "seq", "tensor"))
    n_y = n_seq // 2
    half = rows // 2
    units, part = 2 * NH, 2 * NF
    scale = float(rows * n_dp * n_seq) ** (-0.5)
    upw = up_weight.reshape(units, B, B)
    dnw = down_weight.reshape(units, B, B)
    any_space = pl.BlockSpec(memory_space=pl.ANY)
    vmem = pl.BlockSpec(memory_space=pltpu.VMEM)
    smem = pl.BlockSpec(memory_space=pltpu.SMEM)
    dma = pltpu.SemaphoreType.DMA
    rows_chip = B // (n_dp * n_y)
    small = jax.ShapeDtypeStruct((NH, 2, rows_chip // 2, B), F32)
    results = pl.pallas_call(
        functools.partial(kernel, (n_dp, n_seq, n_t), scale),
        out_shape=(
            jax.ShapeDtypeStruct((rows, width), BF16),
            jax.ShapeDtypeStruct((rows, width), BF16),
            small,
            small,
        ),
        in_specs=[smem, smem, any_space, any_space, any_space, any_space],
        out_specs=(any_space, any_space, vmem, vmem),
        scratch_shapes=[
            pltpu.VMEM((2, 2, units, B, B), BF16),
            [pltpu.VMEM((2, NF, r, B), BF16) for r in SPLIT],
            [pltpu.VMEM((2, NF, r, B), BF16) for r in SPLIT],
            pltpu.VMEM((2, NF, half, B), BF16),
            pltpu.VMEM((2, NF, B, half), BF16),
            pltpu.VMEM((2, NF, half, B), BF16),
            pltpu.VMEM((2, NH, half, B), BF16),
            pltpu.VMEM((2, NH, half, B), BF16),
            pltpu.VMEM((2, 2, half, width), BF16),
            pltpu.VMEM((4, part, B, B), F32),
            pltpu.VMEM((4, part, B, B), BF16),
            pltpu.VMEM((4, part, B, B), BF16),
            pltpu.VMEM((4, n_dp, n_y, part, rows_chip, B), BF16),
            pltpu.VMEM((4, 2, 2, part, rows_chip, B), BF16),
            pltpu.VMEM((4, 2, 2, part, rows_chip, B), BF16),
            pltpu.VMEM((4, 2, 2, part, rows_chip, B), BF16),
            pltpu.VMEM((4, 2, 2, part, rows_chip, B), BF16),
            pltpu.VMEM((4, n_y, part, rows_chip, B), BF16),
            pltpu.VMEM((4, n_y, part, rows_chip, B), F32),
            pltpu.VMEM((4, n_y - 1, part, rows_chip, B), BF16),
            pltpu.VMEM((2, part, rows_chip, B), F32),
            pltpu.VMEM((2, part, rows_chip, B), BF16),
            pltpu.VMEM((2, part, rows_chip, B), BF16),
            pltpu.VMEM((2, part, rows_chip, B), F32),
            pltpu.VMEM((2, part, rows_chip // 2, B), F32),
            pltpu.SMEM((128,), jnp.int32),
            dma((2 + 2 * NF * CHUNKS,)),
            dma((4,)),
            dma((2 * NF * CHUNKS,)),
            dma((2 * NF * CHUNKS,)),
            dma((3 + 12,)),
            dma((16,)),
            dma((16,)),
            dma((16,)),
            dma((2 * CHUNKS,)),
            dma((2 * CHUNKS,)),
            dma((2 * CHUNKS,)),
            dma((32,)),
            dma((32,)),
            dma((3, 4, 2)),
            dma((3, 4, 2)),
            dma((12,)),
            dma((12,)),
            dma((2, 3)),
        ],
        compiler_params=pltpu.CompilerParams(
            collective_id=0, has_side_effects=True, vmem_limit_bytes=60 * 1024 * 1024
        ),
        name="butterfly",
    )(jnp.swapaxes(up_perm, 1, 2), jnp.swapaxes(down_perm, 1, 2), tokens, out_grad, upw, dnw)
    return pl.pallas_call(
        hand_over,
        out_shape=tuple(jax.ShapeDtypeStruct(r.shape, r.dtype) for r in results),
        in_specs=[any_space] * 4,
        out_specs=(any_space,) * 4,
        scratch_shapes=[pltpu.VMEM(r.shape, r.dtype) for r in results] + [dma((4, PIECES, 2))],
        name="results",
    )(*results)


def solution(mesh):
    in_specs = (
        P(("dp", "seq"), "tensor"),
        P(("dp", "seq"), "tensor"),
        P(),
        P(),
        P("tensor", None, None, None),
        P("tensor", None, None, None),
    )
    out_specs = (
        P(("dp", "seq"), "tensor"),
        P(("dp", "seq"), "tensor"),
        P("tensor", None, ("dp", "seq"), None),
        P("tensor", None, ("dp", "seq"), None),
    )
    return jax.shard_map(
        on_device, mesh=mesh, in_specs=in_specs, out_specs=out_specs, check_vma=False
    )
```

```python
import functools
import math

import jax
import jax.numpy as jnp
from jax import lax
from jax.experimental import pallas as pl
from jax.experimental.pallas import tpu as pltpu
from jax.sharding import PartitionSpec as P

F32 = jnp.float32
BF16 = jnp.bfloat16
B = 256
NF = 4
NH = 8
SPLIT = (96, 96, 64)
CHUNKS = len(SPLIT)
PIECES = 4
ROOT = math.sqrt(2.0 / math.pi)
CUBE = 0.044715


def dot(a, b):
    return jnp.dot(a, b, preferred_element_type=F32)


def dot_nt(a, b):
    return lax.dot_general(a, b, (((1,), (1,)), ((), ())), preferred_element_type=F32)


def lanes(block):
    return pl.ds(pl.multiple_of(block * B, B), B)


def loop(count, body):
    lax.fori_loop(0, count, lambda i, c: (body(i), c)[1], 0)


def kernel(
    sizes, scale,
    up_perm, down_perm, tok_hbm, grd_hbm, upw_hbm, dnw_hbm,
    out_ref, ig_ref, gup_ref, gdn_ref,
    w, tcs, gcs, tj, tt, gj, hid, dpre, obuf,
    keep, snd, rcv, s1, rf, rn, cb, rb, s2, f2, r2, f3, zs, zr, fx, fr, table,
    loc_sem, zw_sem, zi_send, zi_recv, ag_send, ag_recv, sb_send, sb_recv,
    zo_send, zo_recv, cs_send, cs_recv, r1_send, r1_recv, r2_send, r2_recv, end_sem,
):
    n_dp, n_seq, n_t = sizes
    n_y = n_seq // 2
    dp, seq, t = lax.axis_index("dp"), lax.axis_index("seq"), lax.axis_index("tensor")
    y, core = seq // 2, lax.rem(seq, 2)
    half = tok_hbm.shape[0] // 2
    upper = t // (n_t // 2)
    keep_off = upper * half
    send_off = half - keep_off

    def chunk(i, offset=0):
        start = sum(SPLIT[:i])
        if isinstance(offset, int):
            return pl.ds(start, SPLIT[i])
        return pl.ds(pl.multiple_of(offset + start, 32), SPLIT[i])

    def peer(d, s, q):
        return {"dp": d, "seq": s, "tensor": q}

    z_peer = peer(dp, seq, lax.rem(t + n_t // 2, n_t))
    sibling = peer(dp, seq + 1 - 2 * core, t)

    def first_peer(k):
        return peer(lax.rem(dp + k * (1 - core), n_dp), lax.rem(seq + 2 * k * core, n_seq), t)

    def second_peer(k):
        return peer(lax.rem(dp + k * core, n_dp), lax.rem(seq + 2 * k * (1 - core), n_seq), t)

    def remote(src, dst, send, recv, device):
        return pltpu.make_async_remote_copy(
            src_ref=src, dst_ref=dst, send_sem=send, recv_sem=recv,
            device_id=device, device_id_type=pl.DeviceIdType.MESH,
        )

    local = [
        pltpu.make_async_copy(upw_hbm, w.at[0, 0], loc_sem.at[0]),
        pltpu.make_async_copy(dnw_hbm, w.at[0, 1], loc_sem.at[1]),
    ]
    for i in range(CHUNKS):
        rows = chunk(i, keep_off)
        for j, (src, dst) in enumerate(((tok_hbm, tcs[i]), (grd_hbm, gcs[i]))):
            for f in range(NF):
                n = (2 * i + j) * NF + f
                local.append(
                    pltpu.make_async_copy(src.at[rows, f * B : (f + 1) * B], dst.at[0, f], loc_sem.at[2 + n])
                )
    for copy in local:
        copy.start()

    barrier = pltpu.get_barrier_semaphore()
    greeted = [z_peer, sibling]
    greeted += [first_peer(k) for k in range(1, n_dp)] + [second_peer(k) for k in range(1, n_y)]
    for device in greeted:
        pl.semaphore_signal(barrier, inc=1, device_id=device, device_id_type=pl.DeviceIdType.MESH)
    pl.semaphore_wait(barrier, len(greeted))

    chip = dp * n_y + y
    hrows = pl.ds(pl.multiple_of(core * (B // 2), B // 2), B // 2)

    def unit(u, part=hrows):
        return w.at[1, :, u, part]

    zw = [
        remote(upw_hbm.at[chip, hrows], w.at[1, 0, chip, hrows], zw_sem.at[0], zw_sem.at[1], z_peer),
        remote(dnw_hbm.at[chip, hrows], w.at[1, 1, chip, hrows], zw_sem.at[2], zw_sem.at[3], z_peer),
    ]
    for copy in zw:
        copy.start()
    zi = []
    for i in range(CHUNKS):
        rows = chunk(i, send_off)
        for j, (src, dst) in enumerate(((tok_hbm, tcs[i]), (grd_hbm, gcs[i]))):
            for f in range(NF):
                n = (2 * i + j) * NF + f
                zi.append(
                    remote(
                        src.at[rows, f * B : (f + 1) * B], dst.at[1, f], zi_send.at[n], zi_recv.at[n], z_peer
                    )
                )
                zi[-1].start()

    def first_copy(k, u):
        return remote(unit(u), unit(u), ag_send.at[k - 1], ag_recv.at[u], first_peer(k))

    def second_copy(m, k, u):
        return remote(unit(u), unit(u), ag_send.at[3 + 3 * m + k - 1], ag_recv.at[u], second_peer(k))

    def sibling_copy(u):
        return remote(unit(u), unit(u), sb_send.at[u], sb_recv.at[u], sibling)

    other = pl.ds(pl.multiple_of((1 - core) * (B // 2), B // 2), B // 2)

    def sibling_arrival(u):
        return remote(unit(u, other), unit(u, other), sb_send.at[u], sb_recv.at[u], sibling)

    def moved(u_dp, u_y, k1, k2):
        a = lax.rem(u_dp + 8 * n_dp - k1 * (1 - core) - k2 * core, n_dp)
        b = lax.rem(u_y + 8 * n_y - k1 * core - k2 * (1 - core), n_y)
        return a * n_y + b

    def fill(n):
        s, run = n // 4, lax.rem(n, 4)
        source = lax.rem(t + (run // 2) * (n_t // 2), n_t) * 2 + lax.rem(run, 2)
        for p, perm in enumerate((up_perm, down_perm)):
            code = jnp.int32(0)
            for j in range(NF):
                block = perm[s, j, source]
                table[(p * 2 + s) * 16 + run * NF + j] = block
                high = lax.div(block, jnp.int32(2))
                low = block - 2 * high
                code = code + j * ((1 + 3 * low) * (1 + 15 * high))
            for f in range(NF):
                table[64 + (p * 2 + s) * 16 + run * NF + f] = lax.rem(lax.div(code, jnp.int32(4**f)), jnp.int32(4))

    loop(8, fill)

    def entry(kind, s, run, n):
        return table[(kind * 2 + s) * 16 + run * NF + n]

    for copy in zw:
        copy.wait_recv()
    for k in range(1, n_dp):
        first_copy(k, chip).start()
    for m in range(n_dp):
        u = moved(dp, y, m, 0)
        if m:
            first_copy(m, u).wait_recv()
        for k in range(1, n_y):
            second_copy(m, k, u).start()
        sibling_copy(u).start()
    for k in range(1, n_y):
        for m in range(n_dp):
            u = moved(dp, y, m, k)
            second_copy(m, k, u).wait_recv()
            sibling_copy(u).start()
    for copy in local:
        copy.wait()
    loop(n_dp * n_y, lambda u: sibling_arrival(u).wait_recv())

    out_copies = []

    def forward(i):
        rows = chunk(i)
        tc, gc = tcs[i], gcs[i]
        for copy in zi[2 * NF * i : 2 * NF * (i + 1)]:
            copy.wait_recv()

        def hidden(n):
            q, h = n // NH, lax.rem(n, NH)
            run, j = n // NF, lax.rem(n, NF)
            a0 = tc[q, entry(0, 0, run, j)]
            a1 = tc[1 - q, entry(0, 1, run, j)]
            v = dot(a0, w[q, 0, 2 * h]) + dot(a1, w[q, 0, 2 * h + 1])
            g0 = gc[q, entry(1, 0, run, j)]
            g1 = gc[1 - q, entry(1, 1, run, j)]
            d = dot_nt(g0, w[q, 1, 2 * h]) + dot_nt(g1, w[q, 1, 2 * h + 1])
            v2 = v * v
            th = jnp.tanh(ROOT * (v + CUBE * (v2 * v)))
            cdf = 0.5 * (1.0 + th)
            hv = (v * cdf).astype(BF16)
            slope = cdf + (0.5 * ROOT) * v * (1.0 - th * th) * (1.0 + (3.0 * CUBE) * v2)
            hid[q, h, rows] = hv
            dpre[q, h, rows] = (d * slope).astype(BF16)

        loop(2 * NH, hidden)

        def join(n):
            x, f = n // NF, lax.rem(n, NF)
            tj[x, f, rows] = tc[x, f]
            gj[x, f, rows] = gc[x, f]

        loop(2 * NF, join)

    def outputs(i, x):
        rows, there = chunk(i), chunk(i, keep_off)

        def block(f):
            acc = jnp.zeros((SPLIT[i], B), F32)
            back = jnp.zeros((SPLIT[i], B), F32)
            for s in range(2):
                q = x if s == 0 else 1 - x
                for r in range(2):
                    h = r * NF + entry(3, s, 2 * q + r, f)
                    acc += dot(hid[q, h, rows], w[q, 1, 2 * h + s])
                    h = r * NF + entry(2, s, 2 * q + r, f)
                    back += dot_nt(dpre[q, h, rows], w[q, 0, 2 * h + s])
            if x == 1:
                obuf[0, rows, lanes(f)] = acc.astype(BF16)
                obuf[1, rows, lanes(f)] = back.astype(BF16)
            else:
                out_ref[there, lanes(f)] = acc.astype(BF16)
                ig_ref[there, lanes(f)] = back.astype(BF16)

        loop(NF, block)
        if x == 1:
            for j, dst in enumerate((out_ref, ig_ref)):
                n = 2 * i + j
                copy = remote(obuf.at[j, rows], dst.at[there], zo_send.at[n], zo_recv.at[n], z_peer)
                copy.start()
                out_copies.append(copy)

    def exchange(i, n):
        return remote(snd.at[i, n], rcv.at[i, n], cs_send.at[8 * i + n], cs_recv.at[8 * i + n], sibling)

    def gradients(i):
        q, r = 1 - i // 2, i % 2
        run = 2 * q + r

        def block(j):
            h = r * NF + j
            hidden_t = hid[q, h].T

            def pair(s):
                x = q * (1 - s) + (1 - q) * s
                return (
                    dot(tt[x, entry(0, s, run, j)], dpre[q, h]),
                    dot(hidden_t, gj[x, entry(1, s, run, j)]),
                )

            gu, gd = pair(1 - core)
            snd[i, j] = gu.astype(BF16)
            snd[i, NF + j] = gd.astype(BF16)
            exchange(i, j).start()
            exchange(i, NF + j).start()
            gu, gd = pair(core)
            keep[i, j] = gu
            keep[i, NF + j] = gd

        loop(NF, block)

    def place(a, b):
        return pl.ds(pl.multiple_of(a * (64 - 48 * core) + b * (16 + 48 * core), 16), 16)

    def summed(i, a, b):
        return keep[i, :, place(a, b), :] + rcv[i, :, place(a, b), :].astype(F32)

    mine_1 = dp * (1 - core) + y * core
    mine_2 = y * (1 - core) + dp * core
    down_1, up_1, far_1 = (lax.rem(mine_1 + k, n_dp) for k in (3, 1, 2))
    halves = pl.ds(0, 2), pl.ds(2, 2)

    def far_copy(i, d):
        return remote(
            s1.at[i, far_1, halves[d]], rf.at[i, d], r1_send.at[0, i, d], r1_recv.at[0, i, d], first_peer(3 - 2 * d)
        )

    def near_copy(i, d):
        return remote(
            s1.at[i, up_1 if d else down_1, halves[1 - d]], rn.at[i, d],
            r1_send.at[1, i, d], r1_recv.at[1, i, d], first_peer(3 - 2 * d),
        )

    def both_copy(i, d):
        return remote(
            cb.at[i, d], rb.at[i, d], r1_send.at[2, i, d], r1_recv.at[2, i, d], first_peer(3 - 2 * d)
        )

    def stage_1(i):
        loop(2 * NF, lambda n: exchange(i, n).wait_recv())

        def part(n):
            a, b = n // n_y, lax.rem(n, n_y)
            s1[i, a, b] = summed(i, a, b).astype(BF16)

        loop(n_dp * n_y, part)
        for d in range(2):
            far_copy(i, d).start()
        for d in range(2):
            near_copy(i, d).start()

    def stage_2(i):
        for d in range(2):
            far_copy(i, d).wait_recv()

            def part(b):
                v = summed(i, up_1 if d else down_1, 2 * d + b) + rf[i, d, b].astype(F32)
                cb[i, d, b] = v.astype(BF16)

            loop(2, part)
            both_copy(i, d).start()

    def stage_3(i):
        for d in range(2):
            near_copy(i, d).wait_recv()
        for d in range(2):
            both_copy(i, d).wait_recv()
        for d in range(2):

            def part(b):
                v = summed(i, mine_1, 2 * d + b) + rb[i, d, b].astype(F32) + rn[i, 1 - d, b].astype(F32)
                f2[i, 2 * d + b] = v
                s2[i, 2 * d + b] = v.astype(BF16)

            loop(2, part)
        for k in range(1, n_y):
            second_axis_copy(i, k).start()

    def second_axis_copy(i, k):
        n = 3 * i + k - 1
        return remote(
            s2.at[i, lax.rem(mine_2 + k, n_y)], r2.at[i, k - 1], r2_send.at[n], r2_recv.at[n], second_peer(k)
        )

    def stage_4(i):
        for k in range(1, n_y):
            second_axis_copy(i, k).wait_recv()
        v = f2[i, mine_2]
        for k in range(n_y - 1):
            v = v + r2[i, k].astype(F32)
        return v

    def return_copy(i):
        return remote(zs.at[i], zr.at[i], end_sem.at[0, i], end_sem.at[1, i], z_peer)

    for i in range(CHUNKS):
        forward(i)
        if i < CHUNKS - 1:
            outputs(i, 1)
            outputs(i, 0)

    def flip(n):
        x, f = n // NF, lax.rem(n, NF)
        tt[x, f] = tj[x, f].T

    loop(2 * NF, flip)
    for i in range(4):
        gradients(i)
        stage_1(i)
        if i:
            stage_2(i - 1)
    outputs(CHUNKS - 1, 1)
    stage_2(3)
    stage_3(0)
    stage_3(1)
    for i in range(2):
        zs[i] = stage_4(i).astype(BF16)
        return_copy(i).start()
    outputs(CHUNKS - 1, 0)
    stage_3(2)
    stage_3(3)
    for i in range(2):
        f3[i] = stage_4(2 + i)
    for i in range(2):
        return_copy(i).wait_recv()
        fx[i] = (f3[i] + zr[i].astype(F32)) * scale
    mine_8 = pl.ds(pl.multiple_of(core * 8, 8), 8)
    their_8 = pl.ds(pl.multiple_of((1 - core) * 8, 8), 8)
    last = remote(fx.at[:, :, their_8], fr, end_sem.at[0, 2], end_sem.at[1, 2], sibling)
    last.start()

    def write_mine(h):
        r, j = h // NF, lax.rem(h, NF)
        gup_ref[h, core] = fx[r, j, mine_8]
        gdn_ref[h, core] = fx[r, NF + j, mine_8]

    loop(NH, write_mine)
    last.wait_recv()

    def write_theirs(h):
        r, j = h // NF, lax.rem(h, NF)
        gup_ref[h, 1 - core] = fr[r, j]
        gdn_ref[h, 1 - core] = fr[r, NF + j]

    loop(NH, write_theirs)

    for copy in out_copies:
        copy.wait()
    for copy in zw + zi:
        copy.wait_send()
    for k in range(1, n_dp):
        first_copy(k, chip).wait_send()
    for m in range(n_dp):
        for k in range(1, n_y):
            second_copy(m, k, chip).wait_send()
    loop(n_dp * n_y, lambda u: sibling_copy(u).wait_send())
    for i in range(4):
        loop(2 * NF, functools.partial(lambda i, n: exchange(i, n).wait_send(), i))
        for d in range(2):
            far_copy(i, d).wait_send()
            near_copy(i, d).wait_send()
            both_copy(i, d).wait_send()
        for k in range(1, n_y):
            second_axis_copy(i, k).wait_send()
    for i in range(2):
        return_copy(i).wait_send()
    last.wait_send()


def hand_over(*refs):
    sources, targets, sem = refs[:4], refs[4:8], refs[8]
    copies = []
    for i in range(4):
        step = sources[i].shape[0] // PIECES
        for p in range(PIECES):
            part = pl.ds(p * step, step)
            copies.append(pltpu.make_async_copy(sources[i].at[part], targets[i].at[part], sem.at[i, p]))
            copies[-1].start()
    for copy in copies:
        copy.wait()


def on_device(tokens, out_grad, up_perm, down_perm, up_weight, down_weight):
    rows, width = tokens.shape
    n_dp, n_seq, n_t = (lax.axis_size(a) for a in ("dp", "seq", "tensor"))
    n_y = n_seq // 2
    half = rows // 2
    units, part = 2 * NH, 2 * NF
    scale = float(rows * n_dp * n_seq) ** (-0.5)
    upw = up_weight.reshape(units, B, B)
    dnw = down_weight.reshape(units, B, B)
    any_space = pl.BlockSpec(memory_space=pl.ANY)
    vmem = pl.BlockSpec(memory_space=pltpu.VMEM)
    smem = pl.BlockSpec(memory_space=pltpu.SMEM)
    dma = pltpu.SemaphoreType.DMA
    rows_chip = B // (n_dp * n_y)
    small = pltpu.VMEM((NH, 2, rows_chip // 2, B), F32)
    results = pl.pallas_call(
        functools.partial(kernel, (n_dp, n_seq, n_t), scale),
        out_shape=(
            pltpu.VMEM((rows, width), BF16),
            pltpu.VMEM((rows, width), BF16),
            small,
            small,
        ),
        in_specs=[smem, smem, any_space, any_space, any_space, any_space],
        out_specs=(vmem,) * 4,
        scratch_shapes=[
            pltpu.VMEM((2, 2, units, B, B), BF16),
            [pltpu.VMEM((2, NF, r, B), BF16) for r in SPLIT],
            [pltpu.VMEM((2, NF, r, B), BF16) for r in SPLIT],
            pltpu.VMEM((2, NF, half, B), BF16),
            pltpu.VMEM((2, NF, B, half), BF16),
            pltpu.VMEM((2, NF, half, B), BF16),
            pltpu.VMEM((2, NH, half, B), BF16),
            pltpu.VMEM((2, NH, half, B), BF16),
            pltpu.VMEM((2, half, width), BF16),
            pltpu.VMEM((4, part, B, B), F32),
            pltpu.VMEM((4, part, B, B), BF16),
            pltpu.VMEM((4, part, B, B), BF16),
            pltpu.VMEM((4, n_dp, n_y, part, rows_chip, B), BF16),
            pltpu.VMEM((4, 2, 2, part, rows_chip, B), BF16),
            pltpu.VMEM((4, 2, 2, part, rows_chip, B), BF16),
            pltpu.VMEM((4, 2, 2, part, rows_chip, B), BF16),
            pltpu.VMEM((4, 2, 2, part, rows_chip, B), BF16),
            pltpu.VMEM((4, n_y, part, rows_chip, B), BF16),
            pltpu.VMEM((4, n_y, part, rows_chip, B), F32),
            pltpu.VMEM((4, n_y - 1, part, rows_chip, B), BF16),
            pltpu.VMEM((2, part, rows_chip, B), F32),
            pltpu.VMEM((2, part, rows_chip, B), BF16),
            pltpu.VMEM((2, part, rows_chip, B), BF16),
            pltpu.VMEM((2, part, rows_chip, B), F32),
            pltpu.VMEM((2, part, rows_chip // 2, B), F32),
            pltpu.SMEM((128,), jnp.int32),
            dma((2 + 2 * NF * CHUNKS,)),
            dma((4,)),
            dma((2 * NF * CHUNKS,)),
            dma((2 * NF * CHUNKS,)),
            dma((3 + 12,)),
            dma((16,)),
            dma((16,)),
            dma((16,)),
            dma((2 * CHUNKS,)),
            dma((2 * CHUNKS,)),
            dma((32,)),
            dma((32,)),
            dma((3, 4, 2)),
            dma((3, 4, 2)),
            dma((12,)),
            dma((12,)),
            dma((2, 3)),
        ],
        compiler_params=pltpu.CompilerParams(
            collective_id=0, has_side_effects=True, vmem_limit_bytes=52 * 1024 * 1024
        ),
        name="butterfly",
    )(jnp.swapaxes(up_perm, 1, 2), jnp.swapaxes(down_perm, 1, 2), tokens, out_grad, upw, dnw)
    results = [pltpu.with_memory_space_constraint(r, pltpu.VMEM) for r in results]
    return pl.pallas_call(
        hand_over,
        out_shape=tuple(jax.ShapeDtypeStruct(r.shape, r.dtype) for r in results),
        in_specs=[vmem] * 4,
        out_specs=(any_space,) * 4,
        scratch_shapes=[dma((4, PIECES))],
        name="results",
    )(*results)


def solution(mesh):
    in_specs = (
        P(("dp", "seq"), "tensor"),
        P(("dp", "seq"), "tensor"),
        P(),
        P(),
        P("tensor", None, None, None),
        P("tensor", None, None, None),
    )
    out_specs = (
        P(("dp", "seq"), "tensor"),
        P(("dp", "seq"), "tensor"),
        P("tensor", None, ("dp", "seq"), None),
        P("tensor", None, ("dp", "seq"), None),
    )
    return jax.shard_map(
        on_device, mesh=mesh, in_specs=in_specs, out_specs=out_specs, check_vma=False
    )
```

```python
import functools
import math

import jax
import jax.numpy as jnp
from jax import lax
from jax.experimental import pallas as pl
from jax.experimental.pallas import tpu as pltpu
from jax.sharding import PartitionSpec as P

F32 = jnp.float32
BF16 = jnp.bfloat16
B = 256
NF = 4
NH = 8
SPLIT = (64, 128, 64)
CHUNKS = len(SPLIT)
PIECES = 1
ROOT = math.sqrt(2.0 / math.pi)
CUBE = 0.044715


def dot(a, b):
    return jnp.dot(a, b, preferred_element_type=F32)


def dot_nt(a, b):
    return lax.dot_general(a, b, (((1,), (1,)), ((), ())), preferred_element_type=F32)


def lanes(block):
    return pl.ds(pl.multiple_of(block * B, B), B)


def loop(count, body):
    lax.fori_loop(0, count, lambda i, c: (body(i), c)[1], 0)


def kernel(
    sizes, scale,
    up_perm, down_perm, tok_hbm, grd_hbm, upw_hbm, dnw_hbm,
    out_ref, ig_ref, gup_ref, gdn_ref,
    w, tcs, gcs, tj, tt, gj, hid, dpre, obuf,
    keep, snd, rcv, s1, rf, rn, cb, rb, s2, f2, r2, f3, zs, zr, fx, fr, table,
    loc_sem, zw_sem, zi_send, zi_recv, ag_send, ag_recv, sb_send, sb_recv,
    zo_send, zo_recv, cs_send, cs_recv, r1_send, r1_recv, r2_send, r2_recv, end_sem,
):
    n_dp, n_seq, n_t = sizes
    n_y = n_seq // 2
    dp, seq, t = lax.axis_index("dp"), lax.axis_index("seq"), lax.axis_index("tensor")
    y, core = seq // 2, lax.rem(seq, 2)
    half = tok_hbm.shape[0] // 2
    upper = t // (n_t // 2)
    keep_off = upper * half
    send_off = half - keep_off

    def chunk(i, offset=0):
        start = sum(SPLIT[:i])
        if isinstance(offset, int):
            return pl.ds(start, SPLIT[i])
        return pl.ds(pl.multiple_of(offset + start, 32), SPLIT[i])

    def peer(d, s, q):
        return {"dp": d, "seq": s, "tensor": q}

    z_peer = peer(dp, seq, lax.rem(t + n_t // 2, n_t))
    sibling = peer(dp, seq + 1 - 2 * core, t)

    def first_peer(k):
        return peer(lax.rem(dp + k * (1 - core), n_dp), lax.rem(seq + 2 * k * core, n_seq), t)

    def second_peer(k):
        return peer(lax.rem(dp + k * core, n_dp), lax.rem(seq + 2 * k * (1 - core), n_seq), t)

    def remote(src, dst, send, recv, device):
        return pltpu.make_async_remote_copy(
            src_ref=src, dst_ref=dst, send_sem=send, recv_sem=recv,
            device_id=device, device_id_type=pl.DeviceIdType.MESH,
        )

    local = [
        pltpu.make_async_copy(upw_hbm, w.at[0, 0], loc_sem.at[0]),
        pltpu.make_async_copy(dnw_hbm, w.at[0, 1], loc_sem.at[1]),
    ]
    for i in range(CHUNKS):
        rows = chunk(i, keep_off)
        for j, (src, dst) in enumerate(((tok_hbm, tcs[i]), (grd_hbm, gcs[i]))):
            for f in range(NF):
                n = (2 * i + j) * NF + f
                local.append(
                    pltpu.make_async_copy(src.at[rows, f * B : (f + 1) * B], dst.at[0, f], loc_sem.at[2 + n])
                )
    for copy in local:
        copy.start()

    barrier = pltpu.get_barrier_semaphore()
    greeted = [z_peer, sibling]
    greeted += [first_peer(k) for k in range(1, n_dp)] + [second_peer(k) for k in range(1, n_y)]
    for device in greeted:
        pl.semaphore_signal(barrier, inc=1, device_id=device, device_id_type=pl.DeviceIdType.MESH)
    pl.semaphore_wait(barrier, len(greeted))

    chip = dp * n_y + y
    hrows = pl.ds(pl.multiple_of(core * (B // 2), B // 2), B // 2)

    def unit(u, part=hrows):
        return w.at[1, :, u, part]

    zw = [
        remote(upw_hbm.at[chip, hrows], w.at[1, 0, chip, hrows], zw_sem.at[0], zw_sem.at[1], z_peer),
        remote(dnw_hbm.at[chip, hrows], w.at[1, 1, chip, hrows], zw_sem.at[2], zw_sem.at[3], z_peer),
    ]
    for copy in zw:
        copy.start()
    zi = []
    for i in range(CHUNKS):
        rows = chunk(i, send_off)
        for j, (src, dst) in enumerate(((tok_hbm, tcs[i]), (grd_hbm, gcs[i]))):
            for f in range(NF):
                n = (2 * i + j) * NF + f
                zi.append(
                    remote(
                        src.at[rows, f * B : (f + 1) * B], dst.at[1, f], zi_send.at[n], zi_recv.at[n], z_peer
                    )
                )
                zi[-1].start()

    def first_copy(k, u):
        return remote(unit(u), unit(u), ag_send.at[k - 1], ag_recv.at[u], first_peer(k))

    def second_copy(m, k, u):
        return remote(unit(u), unit(u), ag_send.at[3 + 3 * m + k - 1], ag_recv.at[u], second_peer(k))

    def sibling_copy(u):
        return remote(unit(u), unit(u), sb_send.at[u], sb_recv.at[u], sibling)

    other = pl.ds(pl.multiple_of((1 - core) * (B // 2), B // 2), B // 2)

    def sibling_arrival(u):
        return remote(unit(u, other), unit(u, other), sb_send.at[u], sb_recv.at[u], sibling)

    def moved(u_dp, u_y, k1, k2):
        a = lax.rem(u_dp + 8 * n_dp - k1 * (1 - core) - k2 * core, n_dp)
        b = lax.rem(u_y + 8 * n_y - k1 * core - k2 * (1 - core), n_y)
        return a * n_y + b

    def fill(n):
        s, run = n // 4, lax.rem(n, 4)
        source = lax.rem(t + (run // 2) * (n_t // 2), n_t) * 2 + lax.rem(run, 2)
        for p, perm in enumerate((up_perm, down_perm)):
            code = jnp.int32(0)
            for j in range(NF):
                block = perm[s, j, source]
                table[(p * 2 + s) * 16 + run * NF + j] = block
                high = lax.div(block, jnp.int32(2))
                low = block - 2 * high
                code = code + j * ((1 + 3 * low) * (1 + 15 * high))
            for f in range(NF):
                table[64 + (p * 2 + s) * 16 + run * NF + f] = lax.rem(lax.div(code, jnp.int32(4**f)), jnp.int32(4))

    loop(8, fill)

    def entry(kind, s, run, n):
        return table[(kind * 2 + s) * 16 + run * NF + n]

    for copy in zw:
        copy.wait_recv()
    for k in range(1, n_dp):
        first_copy(k, chip).start()
    for m in range(n_dp):
        u = moved(dp, y, m, 0)
        if m:
            first_copy(m, u).wait_recv()
        for k in range(1, n_y):
            second_copy(m, k, u).start()
        sibling_copy(u).start()
    for k in range(1, n_y):
        for m in range(n_dp):
            u = moved(dp, y, m, k)
            second_copy(m, k, u).wait_recv()
            sibling_copy(u).start()
    for copy in local:
        copy.wait()
    loop(n_dp * n_y, lambda u: sibling_arrival(u).wait_recv())

    out_copies = []

    def forward(i):
        rows = chunk(i)
        tc, gc = tcs[i], gcs[i]
        for copy in zi[2 * NF * i : 2 * NF * (i + 1)]:
            copy.wait_recv()

        def hidden(n):
            q, h = n // NH, lax.rem(n, NH)
            run, j = n // NF, lax.rem(n, NF)
            a0 = tc[q, entry(0, 0, run, j)]
            a1 = tc[1 - q, entry(0, 1, run, j)]
            v = dot(a0, w[q, 0, 2 * h]) + dot(a1, w[q, 0, 2 * h + 1])
            g0 = gc[q, entry(1, 0, run, j)]
            g1 = gc[1 - q, entry(1, 1, run, j)]
            d = dot_nt(g0, w[q, 1, 2 * h]) + dot_nt(g1, w[q, 1, 2 * h + 1])
            v2 = v * v
            th = jnp.tanh(ROOT * (v + CUBE * (v2 * v)))
            cdf = 0.5 * (1.0 + th)
            hv = (v * cdf).astype(BF16)
            slope = cdf + (0.5 * ROOT) * v * (1.0 - th * th) * (1.0 + (3.0 * CUBE) * v2)
            hid[q, h, rows] = hv
            dpre[q, h, rows] = (d * slope).astype(BF16)

        loop(2 * NH, hidden)

        def join(n):
            x, f = n // NF, lax.rem(n, NF)
            tj[x, f, rows] = tc[x, f]
            gj[x, f, rows] = gc[x, f]

        loop(2 * NF, join)

    def outputs(i, x):
        rows, there = chunk(i), chunk(i, keep_off)

        def block(f):
            acc = jnp.zeros((SPLIT[i], B), F32)
            back = jnp.zeros((SPLIT[i], B), F32)
            for s in range(2):
                q = x if s == 0 else 1 - x
                for r in range(2):
                    h = r * NF + entry(3, s, 2 * q + r, f)
                    acc += dot(hid[q, h, rows], w[q, 1, 2 * h + s])
                    h = r * NF + entry(2, s, 2 * q + r, f)
                    back += dot_nt(dpre[q, h, rows], w[q, 0, 2 * h + s])
            if x == 1:
                obuf[0, rows, lanes(f)] = acc.astype(BF16)
                obuf[1, rows, lanes(f)] = back.astype(BF16)
            else:
                out_ref[there, lanes(f)] = acc.astype(BF16)
                ig_ref[there, lanes(f)] = back.astype(BF16)

        loop(NF, block)
        if x == 1:
            for j, dst in enumerate((out_ref, ig_ref)):
                n = 2 * i + j
                copy = remote(obuf.at[j, rows], dst.at[there], zo_send.at[n], zo_recv.at[n], z_peer)
                copy.start()
                out_copies.append(copy)

    def exchange(i, n):
        return remote(snd.at[i, n], rcv.at[i, n], cs_send.at[8 * i + n], cs_recv.at[8 * i + n], sibling)

    def gradients(i):
        q, r = 1 - i // 2, i % 2
        run = 2 * q + r

        def block(j):
            h = r * NF + j
            hidden_t = hid[q, h].T

            def pair(s):
                x = q * (1 - s) + (1 - q) * s
                return (
                    dot(tt[x, entry(0, s, run, j)], dpre[q, h]),
                    dot(hidden_t, gj[x, entry(1, s, run, j)]),
                )

            gu, gd = pair(1 - core)
            snd[i, j] = gu.astype(BF16)
            snd[i, NF + j] = gd.astype(BF16)
            exchange(i, j).start()
            exchange(i, NF + j).start()
            gu, gd = pair(core)
            keep[i, j] = gu
            keep[i, NF + j] = gd

        loop(NF, block)

    def place(a, b):
        return pl.ds(pl.multiple_of(a * (64 - 48 * core) + b * (16 + 48 * core), 16), 16)

    def summed(i, a, b):
        return keep[i, :, place(a, b), :] + rcv[i, :, place(a, b), :].astype(F32)

    mine_1 = dp * (1 - core) + y * core
    mine_2 = y * (1 - core) + dp * core
    down_1, up_1, far_1 = (lax.rem(mine_1 + k, n_dp) for k in (3, 1, 2))
    halves = pl.ds(0, 2), pl.ds(2, 2)

    def far_copy(i, d):
        return remote(
            s1.at[i, far_1, halves[d]], rf.at[i, d], r1_send.at[0, i, d], r1_recv.at[0, i, d], first_peer(3 - 2 * d)
        )

    def near_copy(i, d):
        return remote(
            s1.at[i, up_1 if d else down_1, halves[1 - d]], rn.at[i, d],
            r1_send.at[1, i, d], r1_recv.at[1, i, d], first_peer(3 - 2 * d),
        )

    def both_copy(i, d):
        return remote(
            cb.at[i, d], rb.at[i, d], r1_send.at[2, i, d], r1_recv.at[2, i, d], first_peer(3 - 2 * d)
        )

    def stage_1(i):
        loop(2 * NF, lambda n: exchange(i, n).wait_recv())

        def part(n):
            a, b = n // n_y, lax.rem(n, n_y)
            s1[i, a, b] = summed(i, a, b).astype(BF16)

        loop(n_dp * n_y, part)
        for d in range(2):
            far_copy(i, d).start()
        for d in range(2):
            near_copy(i, d).start()

    def stage_2(i):
        for d in range(2):
            far_copy(i, d).wait_recv()

            def part(b):
                v = summed(i, up_1 if d else down_1, 2 * d + b) + rf[i, d, b].astype(F32)
                cb[i, d, b] = v.astype(BF16)

            loop(2, part)
            both_copy(i, d).start()

    def stage_3(i):
        for d in range(2):
            near_copy(i, d).wait_recv()
        for d in range(2):
            both_copy(i, d).wait_recv()
        for d in range(2):

            def part(b):
                v = summed(i, mine_1, 2 * d + b) + rb[i, d, b].astype(F32) + rn[i, 1 - d, b].astype(F32)
                f2[i, 2 * d + b] = v
                s2[i, 2 * d + b] = v.astype(BF16)

            loop(2, part)
        for k in range(1, n_y):
            second_axis_copy(i, k).start()

    def second_axis_copy(i, k):
        n = 3 * i + k - 1
        return remote(
            s2.at[i, lax.rem(mine_2 + k, n_y)], r2.at[i, k - 1], r2_send.at[n], r2_recv.at[n], second_peer(k)
        )

    def stage_4(i):
        for k in range(1, n_y):
            second_axis_copy(i, k).wait_recv()
        v = f2[i, mine_2]
        for k in range(n_y - 1):
            v = v + r2[i, k].astype(F32)
        return v

    def return_copy(i):
        return remote(zs.at[i], zr.at[i], end_sem.at[0, i], end_sem.at[1, i], z_peer)

    for i in range(CHUNKS):
        forward(i)
        if i < CHUNKS - 1:
            outputs(i, 1)
            outputs(i, 0)

    def flip(n):
        x, f = n // NF, lax.rem(n, NF)
        tt[x, f] = tj[x, f].T

    loop(2 * NF, flip)
    for i in range(4):
        gradients(i)
        stage_1(i)
        if i:
            stage_2(i - 1)
    outputs(CHUNKS - 1, 1)
    stage_2(3)
    stage_3(0)
    stage_3(1)
    for i in range(2):
        zs[i] = stage_4(i).astype(BF16)
        return_copy(i).start()
    outputs(CHUNKS - 1, 0)
    stage_3(2)
    stage_3(3)
    for i in range(2):
        f3[i] = stage_4(2 + i)
    for copy in zw + zi:
        copy.wait_send()
    for k in range(1, n_dp):
        first_copy(k, chip).wait_send()
    for m in range(n_dp):
        for k in range(1, n_y):
            second_copy(m, k, chip).wait_send()
    loop(n_dp * n_y, lambda u: sibling_copy(u).wait_send())
    for i in range(4):
        loop(2 * NF, functools.partial(lambda i, n: exchange(i, n).wait_send(), i))
        for d in range(2):
            far_copy(i, d).wait_send()
            near_copy(i, d).wait_send()
            both_copy(i, d).wait_send()
        for k in range(1, n_y):
            second_axis_copy(i, k).wait_send()
    for i in range(2):
        return_copy(i).wait_recv()
        fx[i] = (f3[i] + zr[i].astype(F32)) * scale
    mine_8 = pl.ds(pl.multiple_of(core * 8, 8), 8)
    their_8 = pl.ds(pl.multiple_of((1 - core) * 8, 8), 8)
    last = remote(fx.at[:, :, their_8], fr, end_sem.at[0, 2], end_sem.at[1, 2], sibling)
    last.start()

    def write_mine(h):
        r, j = h // NF, lax.rem(h, NF)
        gup_ref[h, core] = fx[r, j, mine_8]
        gdn_ref[h, core] = fx[r, NF + j, mine_8]

    loop(NH, write_mine)
    for copy in out_copies:
        copy.wait()
    for i in range(2):
        return_copy(i).wait_send()
    last.wait()

    def write_theirs(h):
        r, j = h // NF, lax.rem(h, NF)
        gup_ref[h, 1 - core] = fr[r, j]
        gdn_ref[h, 1 - core] = fr[r, NF + j]

    loop(NH, write_theirs)


def hand_over(*refs):
    sources, targets, sem = refs[:4], refs[4:8], refs[8]
    copies = []
    for i in range(4):
        step = sources[i].shape[0] // PIECES
        for p in range(PIECES):
            part = pl.ds(p * step, step)
            copies.append(pltpu.make_async_copy(sources[i].at[part], targets[i].at[part], sem.at[i, p]))
            copies[-1].start()
    for copy in copies:
        copy.wait()


def on_device(tokens, out_grad, up_perm, down_perm, up_weight, down_weight):
    rows, width = tokens.shape
    n_dp, n_seq, n_t = (lax.axis_size(a) for a in ("dp", "seq", "tensor"))
    n_y = n_seq // 2
    half = rows // 2
    units, part = 2 * NH, 2 * NF
    scale = float(rows * n_dp * n_seq) ** (-0.5)
    upw = up_weight.reshape(units, B, B)
    dnw = down_weight.reshape(units, B, B)
    any_space = pl.BlockSpec(memory_space=pl.ANY)
    vmem = pl.BlockSpec(memory_space=pltpu.VMEM)
    smem = pl.BlockSpec(memory_space=pltpu.SMEM)
    dma = pltpu.SemaphoreType.DMA
    rows_chip = B // (n_dp * n_y)
    small = pltpu.VMEM((NH, 2, rows_chip // 2, B), F32)
    results = pl.pallas_call(
        functools.partial(kernel, (n_dp, n_seq, n_t), scale),
        out_shape=(
            pltpu.VMEM((rows, width), BF16),
            pltpu.VMEM((rows, width), BF16),
            small,
            small,
        ),
        in_specs=[smem, smem, any_space, any_space, any_space, any_space],
        out_specs=(vmem,) * 4,
        scratch_shapes=[
            pltpu.VMEM((2, 2, units, B, B), BF16),
            [pltpu.VMEM((2, NF, r, B), BF16) for r in SPLIT],
            [pltpu.VMEM((2, NF, r, B), BF16) for r in SPLIT],
            pltpu.VMEM((2, NF, half, B), BF16),
            pltpu.VMEM((2, NF, B, half), BF16),
            pltpu.VMEM((2, NF, half, B), BF16),
            pltpu.VMEM((2, NH, half, B), BF16),
            pltpu.VMEM((2, NH, half, B), BF16),
            pltpu.VMEM((2, half, width), BF16),
            pltpu.VMEM((4, part, B, B), F32),
            pltpu.VMEM((4, part, B, B), BF16),
            pltpu.VMEM((4, part, B, B), BF16),
            pltpu.VMEM((4, n_dp, n_y, part, rows_chip, B), BF16),
            pltpu.VMEM((4, 2, 2, part, rows_chip, B), BF16),
            pltpu.VMEM((4, 2, 2, part, rows_chip, B), BF16),
            pltpu.VMEM((4, 2, 2, part, rows_chip, B), BF16),
            pltpu.VMEM((4, 2, 2, part, rows_chip, B), BF16),
            pltpu.VMEM((4, n_y, part, rows_chip, B), BF16),
            pltpu.VMEM((4, n_y, part, rows_chip, B), F32),
            pltpu.VMEM((4, n_y - 1, part, rows_chip, B), BF16),
            pltpu.VMEM((2, part, rows_chip, B), F32),
            pltpu.VMEM((2, part, rows_chip, B), BF16),
            pltpu.VMEM((2, part, rows_chip, B), BF16),
            pltpu.VMEM((2, part, rows_chip, B), F32),
            pltpu.VMEM((2, part, rows_chip // 2, B), F32),
            pltpu.SMEM((128,), jnp.int32),
            dma((2 + 2 * NF * CHUNKS,)),
            dma((4,)),
            dma((2 * NF * CHUNKS,)),
            dma((2 * NF * CHUNKS,)),
            dma((3 + 12,)),
            dma((16,)),
            dma((16,)),
            dma((16,)),
            dma((2 * CHUNKS,)),
            dma((2 * CHUNKS,)),
            dma((32,)),
            dma((32,)),
            dma((3, 4, 2)),
            dma((3, 4, 2)),
            dma((12,)),
            dma((12,)),
            dma((2, 3)),
        ],
        compiler_params=pltpu.CompilerParams(
            collective_id=0, has_side_effects=True, vmem_limit_bytes=52 * 1024 * 1024
        ),
        name="butterfly",
    )(jnp.swapaxes(up_perm, 1, 2), jnp.swapaxes(down_perm, 1, 2), tokens, out_grad, upw, dnw)
    results = [pltpu.with_memory_space_constraint(r, pltpu.VMEM) for r in results]
    return pl.pallas_call(
        hand_over,
        out_shape=tuple(jax.ShapeDtypeStruct(r.shape, r.dtype) for r in results),
        in_specs=[vmem] * 4,
        out_specs=(any_space,) * 4,
        scratch_shapes=[dma((4, PIECES))],
        name="results",
    )(*results)


def solution(mesh):
    in_specs = (
        P(("dp", "seq"), "tensor"),
        P(("dp", "seq"), "tensor"),
        P(),
        P(),
        P("tensor", None, None, None),
        P("tensor", None, None, None),
    )
    out_specs = (
        P(("dp", "seq"), "tensor"),
        P(("dp", "seq"), "tensor"),
        P("tensor", None, ("dp", "seq"), None),
        P("tensor", None, ("dp", "seq"), None),
    )
    return jax.shard_map(
        on_device, mesh=mesh, in_specs=in_specs, out_specs=out_specs, check_vma=False
    )
```
